32 devices in a mesh: book: 2 (over y), seq: 4 (over x, core), sub: 4 (over z).
Axes of the slice: x: 2, y: 2, z: 4, core: 2. Of those that a mesh axis runs over, the one named last changes fastest.
Arguments:
- queries: bfloat16 [16384, 2048], P(('book', 'seq'), 'sub'), parts along dimension 0, may hold values from -4 to 1920
- keys: bfloat16 [16384, 2048], P(('book', 'seq'), 'sub'), parts along dimension 0, may hold values from -6 to 4
- values: bfloat16 [16384, 2048], P(('book', 'seq'), 'sub'), parts along dimension 0, may hold values from -6 to 6
- decay: float32 [8, 8], P('book', 'sub'), parts along dimension 0, may hold values from 0.05 to 1
- gate: float32 [8], P('sub'), may hold values from -0.5 to 3
- summary: bfloat16 [512, 2048], P(('book', 'seq')), parts along dimension 0, may hold values from -6 to 6
- wq_sum: bfloat16 [2048, 2048], P(None, 'sub'), may hold values from -0.25 to 0.25
- wo_sum: bfloat16 [2048, 2048], P('sub'), may hold values from -0.125 to 0.125
Outputs:
- attended: bfloat16 [16384, 2048], P(('book', 'seq'), 'sub'), parts along dimension 0
- summarized: bfloat16 [512, 2048], P(('book', 'seq')), parts along dimension 0
The draws below stay inside these ranges and needn't reach their ends.
There are 2 independent parts, one for each index of `book`. The reference program is written for one: setup_inputs(seed, part) draws one part's arguments, and reference() takes and returns one part's arrays. A program takes and returns all parts, laid end to end along the dimension named above; an argument that names none is the same for every part. Nothing has to cross between parts.
All inputs are finite; a program needn't handle non-finite values.
Results may differ from the reference program's by a relative error of at most 0.019.
Values may be sent and summed in bfloat16 or wider, within the bound.
No kernel may reach another device: no remote copies, remote signals or barrier semaphores. Data moves between devices by JAX's collectives and lax.ppermute only.
A program may use at most 128 MiB of HBM per device.

```python
import jax
import jax.numpy as jnp
from jax import lax

D = 2048
HEAD_TOTAL = 8
DH = 256
SEG = 2048
STEPS = 4
SEGMENT_TOTAL = 4
TOKENS = 8192
SUMROWS = 256


def query_key_couple(key):
    keys_split = jax.random.split(jax.random.fold_in(key, 11), 4)
    head_shape = (TOKENS, HEAD_TOTAL, DH)
    chosen = jax.random.randint(keys_split[0], (TOKENS, HEAD_TOTAL), 0, DH)
    hot_mask = jnp.arange(DH)[None, None, :] == chosen[:, :, None]
    amplitude = jax.random.uniform(keys_split[1], head_shape, jnp.float32, 1.0, 4.0)
    cold_part = jnp.clip(-5.5 + 0.25 * jax.random.normal(keys_split[2], head_shape, jnp.float32), -6.0, -5.0)
    query_draw = jnp.clip(jax.random.normal(keys_split[3], head_shape, jnp.float32), -4.0, 4.0)
    key_draw = jnp.where(hot_mask, amplitude, cold_part)
    return (query_draw.reshape(TOKENS, HEAD_TOTAL * DH), key_draw.reshape(TOKENS, HEAD_TOTAL * DH))


def draw_queries(key, part):
    return query_key_couple(key)[0].astype(jnp.bfloat16)


def draw_keys(key, part):
    return query_key_couple(key)[1].astype(jnp.bfloat16)


def draw_decay(key, part):
    every_key_row = jax.random.split(jax.random.fold_in(key, 23), 5)
    fast_level = 4
    fast_heads = jax.random.randint(every_key_row[0], (HEAD_TOTAL,), 0, 8) < fast_level
    slow_rate = jnp.exp(jnp.log(0.5) / SEGMENT_TOTAL * jax.random.uniform(every_key_row[1], (SEGMENT_TOTAL, HEAD_TOTAL), jnp.float32, 0.5, 1.5))
    fast_rate = jax.random.uniform(every_key_row[2], (SEGMENT_TOTAL, HEAD_TOTAL), jnp.float32, 0.1, 0.4)
    decay_speed = jnp.where(fast_heads[None, :], fast_rate, slow_rate)
    sudden_spike = jax.random.randint(every_key_row[3], (SEGMENT_TOTAL, 1), 0, SEGMENT_TOTAL) < 3
    spike_factor = jax.random.uniform(every_key_row[4], (SEGMENT_TOTAL, HEAD_TOTAL), jnp.float32, 0.5, 0.8)
    return jnp.where(sudden_spike, decay_speed * spike_factor, decay_speed).astype(jnp.float32)


def block_levels(rng, dims, cuts, smallest, high):
    loudness = 1.0
    for axis_at, blocks in cuts:
        draws = jax.random.uniform(jax.random.fold_in(jax.random.fold_in(rng, 6), axis_at), (blocks,), jnp.float32, smallest / len(cuts), high / len(cuts))
        loudness = loudness * jnp.repeat(jnp.exp(draws), dims[axis_at] // blocks).reshape((-1,) + (1,) * (len(dims) - 1 - axis_at))
    return loudness


def normal_values(rng, extent, scale, bound, shards=(), kind=jnp.bfloat16):
    loudness = block_levels(rng, extent, shards, -0.22, 0.18) if shards else 1.0
    drawn = jax.random.normal(rng, extent, jnp.float32) * scale * loudness
    return jnp.minimum(jnp.maximum(drawn, -bound), bound).astype(kind)


def setup_inputs(seed: int = 0, part: int = 0) -> dict:
    streams_of = jax.random.split(jax.random.key(seed), 9)
    part_keys = jax.random.split(jax.random.fold_in(streams_of[8], part), 9)
    return {
        "queries": draw_queries(jax.random.fold_in(jax.random.fold_in(streams_of[8], part), 71), part),
        "keys": draw_keys(jax.random.fold_in(jax.random.fold_in(streams_of[8], part), 71), part),
        "values": normal_values(part_keys[2], (TOKENS, HEAD_TOTAL * DH), 1.0, 6.0, ((0, 4), (1, 4))),
        "decay": draw_decay(jax.random.fold_in(jax.random.fold_in(streams_of[8], part), 71), part),
        "gate": jnp.clip(-0.5 + 3.5 * jax.random.uniform(streams_of[4], (HEAD_TOTAL,), jnp.float32) ** block_levels(streams_of[4], (HEAD_TOTAL,), ((0, 4),), -0.2, 0.2), -0.5, 3.0),
        "summary": normal_values(part_keys[5], (SUMROWS, D), 1.0, 6.0, ((0, 4),)),
        "wq_sum": normal_values(streams_of[6], (D, HEAD_TOTAL * DH), (D // 4) ** -0.5, 0.25, ((1, 4),)),
        "wo_sum": normal_values(streams_of[7], (HEAD_TOTAL * DH, D), (HEAD_TOTAL * DH) ** -0.5, 0.125, ((0, 4),)),
    }


top_precision = lax.Precision.HIGHEST

def feature_map(inputs):
    return jax.nn.elu(inputs) + 1.0

def head_rms(inputs):
    return inputs * lax.rsqrt(lax.optimization_barrier(jnp.mean(inputs * inputs, axis=-1, keepdims=True)) + 1e-06)

def memory_read(lifted, memory, normalizer):
    numerator = jnp.einsum('qhd,hde->qhe', lifted, memory, precision=top_precision)
    denominator = jnp.einsum('qhd,hd->qh', lifted, normalizer, precision=top_precision) + 1.0
    return numerator / denominator[..., None]

def plain_attention(q_part, k_part, v_part):
    length = q_part.shape[0]
    scores = jnp.einsum('qhd,khd->hqk', q_part.astype(jnp.float32), k_part.astype(jnp.float32)) * q_part.shape[2] ** (-0.5)
    positions = jnp.arange(length)
    scores = jnp.where(positions[None, None, :] <= positions[None, :, None], scores, -jnp.inf)
    weights = jax.nn.softmax(scores, axis=-1).astype(jnp.bfloat16)
    return jnp.einsum('hqk,khd->qhd', weights.astype(jnp.float32), v_part.astype(jnp.float32))

def reference(queries, keys, values, decay, gate, summary, wq_sum, wo_sum):
    q_seg = queries.reshape(SEGMENT_TOTAL, SEG, HEAD_TOTAL, DH)
    k_seg = keys.reshape(SEGMENT_TOTAL, SEG, HEAD_TOTAL, DH)
    v_seg = values.reshape(SEGMENT_TOTAL, SEG, HEAD_TOTAL, DH)
    blend_weight = jax.nn.sigmoid(gate)[None, :, None]

    def one_segment(running, inputs_now):
        memory, normalizer = running
        q_part, k_part, v_part, seg_decay = inputs_now
        recalled = memory_read(feature_map(q_part.astype(jnp.float32)), memory, normalizer)
        local_out = plain_attention(q_part, k_part, v_part)
        mixed = head_rms(blend_weight * recalled + (1.0 - blend_weight) * local_out).astype(jnp.bfloat16)
        lifted_keys = feature_map(k_part.astype(jnp.float32))
        update = jnp.einsum('qhd,qhe->hde', lifted_keys, v_part.astype(jnp.float32), precision=top_precision)
        memory = seg_decay[:, None, None] * memory + update
        normalizer = seg_decay[:, None] * normalizer + lax.optimization_barrier(jnp.sum(lifted_keys, axis=0))
        return ((memory, normalizer), mixed)
    start_state = (jnp.zeros((HEAD_TOTAL, DH, DH), jnp.float32), jnp.zeros((HEAD_TOTAL, DH), jnp.float32))
    (final_memory, final_norm), attended = lax.scan(one_segment, start_state, (q_seg, k_seg, v_seg, decay))
    attended = attended.reshape(TOKENS, HEAD_TOTAL * DH)
    summary_state = summary
    row_count = summary.shape[0]
    for decode_step in range(STEPS):
        lifted = feature_map(jnp.dot(summary_state, wq_sum, preferred_element_type=jnp.float32).reshape(row_count, HEAD_TOTAL, DH))
        recalled = head_rms(memory_read(lifted, final_memory, final_norm)).astype(jnp.bfloat16)
        update = jnp.dot(recalled.reshape(row_count, HEAD_TOTAL * DH), wo_sum, preferred_element_type=jnp.float32)
        summary_state = (summary_state.astype(jnp.float32) + update).astype(jnp.bfloat16)
    return (attended, summary_state)
```

```python
import functools

import jax
import jax.numpy as jnp
from jax import lax
from jax.experimental import pallas as pl
from jax.experimental.pallas import tpu as pltpu
from jax.sharding import PartitionSpec as P

SEG = 2048
STEPS = 4
EPS = 1e-06
LOG2E = 1.4426950408889634
PAD = 16


def lift(x):
    return jnp.where(x > 0.0, x + 1.0, jnp.exp(jnp.minimum(x, 0.0)))


def dot(a, b, dims):
    return lax.dot_general(a, b, (dims, ((), ())), preferred_element_type=jnp.float32)


def update_kernel(heads, width, k_ref, v_ref, u_ref, acc, norm):
    step = pl.program_id(0)

    @pl.when(step == 0)
    def _():
        acc[...] = jnp.zeros_like(acc)
        norm[...] = jnp.zeros_like(norm)

    for h in range(heads):
        cols = slice(h * width, (h + 1) * width)
        lifted = lift(k_ref[:, cols].astype(jnp.float32))
        norm[h, 0:1, :] += jnp.sum(lifted, axis=0, keepdims=True)
        acc[h] += dot(lifted.astype(jnp.bfloat16), v_ref[:, cols], ((0,), (0,)))

    @pl.when(step == pl.num_programs(0) - 1)
    def _():
        for h in range(heads):
            u_ref[h, :width, :] = acc[h].astype(jnp.bfloat16)
            u_ref[h, width:, :] = jnp.broadcast_to(norm[h, 0:1, :], (PAD, width)).astype(
                jnp.bfloat16
            )


def memory_update(keys, values, heads, width):
    rows = keys.shape[0]
    block = 512
    return pl.pallas_call(
        functools.partial(update_kernel, heads, width),
        grid=(rows // block,),
        in_specs=[pl.BlockSpec((block, heads * width), lambda i: (i, 0))] * 2,
        out_specs=pl.BlockSpec((heads, width + PAD, width), lambda i: (0, 0, 0)),
        out_shape=jax.ShapeDtypeStruct((heads, width + PAD, width), jnp.bfloat16),
        scratch_shapes=[
            pltpu.VMEM((heads, width, width), jnp.float32),
            pltpu.VMEM((heads, 8, width), jnp.float32),
        ],
        compiler_params=pltpu.CompilerParams(vmem_limit_bytes=16 << 20),
        cost_estimate=pl.CostEstimate(
            flops=2 * rows * heads * width * width,
            transcendentals=rows * heads * width,
            bytes_accessed=4 * rows * heads * width,
        ),
    )(keys, values)


def attention_kernel(heads, width, first, tile, gate_ref, q_ref, k_ref, v_ref, m_ref, *rest):
    o_ref = rest[-1]
    rows = q_ref.shape[0]
    factor = LOG2E * width ** (-0.5)
    blocks = (first + rows) // tile
    row = lax.broadcasted_iota(jnp.int32, (rows, tile), 0)
    col = lax.broadcasted_iota(jnp.int32, (rows, tile), 1)
    for h in range(heads):
        cols = slice(h * width, (h + 1) * width)
        q = q_ref[:, cols]
        scores = []
        for j in range(blocks):
            s = dot(q, k_ref[j * tile : (j + 1) * tile, cols], ((1,), (1,))) * factor
            if (j + 1) * tile > first + 1:
                s = jnp.where(col + j * tile <= row + first, s, -jnp.inf)
            scores.append(s)
        top = scores[0]
        for s in scores[1:]:
            top = jnp.maximum(top, s)
        top = jnp.max(top, axis=1, keepdims=True)
        total = jnp.zeros((rows, 1), jnp.float32)
        mixed = jnp.zeros((rows, width), jnp.float32)
        for j in range(blocks):
            p = jnp.exp2(scores[j] - top)
            total += jnp.sum(p, axis=1, keepdims=True)
            mixed += dot(p.astype(jnp.bfloat16), v_ref[j * tile : (j + 1) * tile, cols], ((1,), (0,)))
        lifted = lift(q.astype(jnp.float32)).astype(jnp.bfloat16)
        numerator = dot(lifted, m_ref[h, :width, :], ((1,), (0,)))
        norm = m_ref[h, width : width + 1, :].astype(jnp.float32)
        denominator = jnp.sum(lifted.astype(jnp.float32) * norm, axis=1, keepdims=True) + 1.0
        blend = 1.0 / (1.0 + jnp.exp(jnp.full((1, 1), -gate_ref[h], jnp.float32)))
        mixed = mixed * ((1.0 - blend) / total) + numerator * (blend / denominator)
        mean = jnp.mean(mixed * mixed, axis=1, keepdims=True)
        o_ref[:, cols] = (mixed * lax.rsqrt(mean + EPS)).astype(jnp.bfloat16)


def attention_piece(q, k, v, memory, gate, out, heads, width, first, rows):
    total, lanes = q.shape
    span = first + rows
    row_spec = pl.BlockSpec((rows, lanes), lambda i: (first // rows, 0))
    span_spec = pl.BlockSpec((span, lanes), lambda i: (0, 0))
    args = [gate, q, k, v, memory]
    specs = [
        pl.BlockSpec(memory_space=pltpu.SMEM),
        row_spec,
        span_spec,
        span_spec,
        pl.BlockSpec(memory.shape, lambda i: (0, 0, 0)),
    ]
    aliases = {}
    if out is not None:
        args.append(out)
        specs.append(pl.BlockSpec(memory_space=pl.ANY))
        aliases = {5: 0}
    return pl.pallas_call(
        functools.partial(attention_kernel, heads, width, first, 512),
        grid=(1,),
        in_specs=specs,
        out_specs=row_spec,
        out_shape=jax.ShapeDtypeStruct((total, lanes), jnp.bfloat16),
        input_output_aliases=aliases,
        compiler_params=pltpu.CompilerParams(vmem_limit_bytes=40 << 20),
        cost_estimate=pl.CostEstimate(
            flops=4 * rows * span * lanes,
            transcendentals=rows * span * heads,
            bytes_accessed=2 * lanes * (2 * rows + 2 * span),
        ),
    )(*args)


def step_kernel(heads, width, parts, *refs):
    state_refs, (wq_ref, wo_ref, m_ref), out_refs = refs[:parts], refs[parts : parts + 3], refs[parts + 3 :]
    size = state_refs[0].shape[0]
    state = jnp.concatenate([r[...] for r in state_refs], axis=0)
    reads = []
    for h in range(heads):
        cols = slice(h * width, (h + 1) * width)
        lifted = lift(dot(state, wq_ref[:, cols], ((1,), (0,)))).astype(jnp.bfloat16)
        numerator = dot(lifted, m_ref[h, :width, :], ((1,), (0,)))
        norm = m_ref[h, width : width + 1, :].astype(jnp.float32)
        denominator = jnp.sum(lifted.astype(jnp.float32) * norm, axis=1, keepdims=True) + 1.0
        read = numerator / denominator
        mean = jnp.mean(read * read, axis=1, keepdims=True)
        reads.append((read * lax.rsqrt(mean + EPS)).astype(jnp.bfloat16))
    partial = dot(jnp.concatenate(reads, axis=1), wo_ref[...], ((1,), (0,)))
    for j in range(parts):
        out_refs[j][...] = partial[j * size : (j + 1) * size].astype(jnp.bfloat16)


def summary_step(pieces, wq, wo, memory, heads, width):
    parts = len(pieces)
    shape = pieces[0].shape
    rows = parts * shape[0]
    return pl.pallas_call(
        functools.partial(step_kernel, heads, width, parts),
        in_specs=[pl.BlockSpec(memory_space=pltpu.VMEM)] * (parts + 3),
        out_specs=[pl.BlockSpec(memory_space=pltpu.VMEM)] * parts,
        out_shape=[jax.ShapeDtypeStruct(shape, jnp.bfloat16)] * parts,
        compiler_params=pltpu.CompilerParams(vmem_limit_bytes=16 << 20),
        cost_estimate=pl.CostEstimate(
            flops=2 * rows * (wq.size + wo.size),
            transcendentals=rows * heads * width,
            bytes_accessed=2 * (wq.size + wo.size) + 4 * rows * shape[1],
        ),
    )(*pieces, wq, wo, memory)


def partner(x, axis, flip):
    return lax.ppermute(x, axis, [(i, i ^ flip) for i in range(lax.axis_size(axis))])


def scan_memory(own, decay, axis):
    count, me = lax.axis_size(axis), lax.axis_index(axis)
    shape = own.shape
    total, prior = own, jnp.zeros_like(own)
    order = jnp.arange(count)
    level = 1
    while level < count:
        mine = (order // level) == (me // level)
        theirs = (order // level) == ((me ^ level) // level)

        def product(mask):
            return jnp.prod(jnp.where(mask[:, None], decay, 1.0), axis=0)[:, None, None]

        got = partner(total, axis, level).astype(jnp.float32)
        later = (me & level) != 0
        before_me = product(mine & (order < me))
        kept = total.astype(jnp.float32)
        prior = jnp.where(later, before_me * got + prior.astype(jnp.float32), prior.astype(jnp.float32)).astype(
            jnp.bfloat16
        )
        total = jnp.where(later, product(mine) * got + kept, product(theirs) * kept + got).astype(jnp.bfloat16)
        level *= 2
    return total, prior


def on_device(queries, keys, values, decay, gate, summary, wq_sum, wo_sum):
    heads = gate.shape[0]
    width = queries.shape[1] // heads
    parts, me = lax.axis_size("sub"), lax.axis_index("sub")

    own = memory_update(keys, values, heads, width)
    final, prior = scan_memory(own, decay, "seq")

    piece_rows = summary.shape[0] // parts
    pieces = [
        lax.dynamic_slice_in_dim(summary, (me ^ j) * piece_rows, piece_rows, 0) for j in range(parts)
    ]
    attended = None
    chunk = 512
    firsts = list(range(0, SEG, chunk))
    for step in range(STEPS):
        partial = summary_step(pieces, wq_sum, wo_sum, final, heads, width)
        got = [partner(partial[j], "sub", j) for j in range(parts - 1, 0, -1)]
        if step < len(firsts):
            attended = attention_piece(
                queries, keys, values, prior, gate, attended, heads, width, firsts[step], chunk
            )
        new = pieces[0].astype(jnp.float32) + partial[0].astype(jnp.float32)
        for g in got:
            new = new + g.astype(jnp.float32)
        new = new.astype(jnp.bfloat16)
        pieces = [new] + [partner(new, "sub", j) for j in range(parts - 1, 0, -1)][::-1]
    out = jnp.zeros_like(summary)
    for j in range(parts):
        out = lax.dynamic_update_slice_in_dim(out, pieces[j], (me ^ j) * piece_rows, 0)
    return (attended, out)


def solution(mesh):
    placed = (
        P(("book", "seq"), "sub"),
        P(("book", "seq"), "sub"),
        P(("book", "seq"), "sub"),
        P("book", "sub"),
        P("sub"),
        P(("book", "seq"), None),
        P(None, "sub"),
        P("sub", None),
    )
    return jax.shard_map(
        on_device,
        mesh=mesh,
        in_specs=placed,
        out_specs=(P(("book", "seq"), "sub"), P(("book", "seq"), None)),
        check_vma=False,
    )
```

```python
import functools

import jax
import jax.numpy as jnp
from jax import lax
from jax.experimental import pallas as pl
from jax.experimental.pallas import tpu as pltpu
from jax.sharding import PartitionSpec as P

SEG = 2048
STEPS = 4
EPS = 1e-06
LOG2E = 1.4426950408889634
PAD = 16


def lift(x):
    return jnp.where(x > 0.0, x + 1.0, jnp.exp(jnp.minimum(x, 0.0)))


def dot(a, b, dims):
    return lax.dot_general(a, b, (dims, ((), ())), preferred_element_type=jnp.float32)


def update_kernel(heads, width, k_ref, v_ref, u_ref, acc, norm):
    step = pl.program_id(0)

    @pl.when(step == 0)
    def _():
        acc[...] = jnp.zeros_like(acc)
        norm[...] = jnp.zeros_like(norm)

    for h in range(heads):
        cols = slice(h * width, (h + 1) * width)
        lifted = lift(k_ref[:, cols].astype(jnp.float32))
        norm[h, 0:1, :] += jnp.sum(lifted, axis=0, keepdims=True)
        acc[h] += dot(lifted.astype(jnp.bfloat16), v_ref[:, cols], ((0,), (0,)))

    @pl.when(step == pl.num_programs(0) - 1)
    def _():
        for h in range(heads):
            u_ref[h, :width, :] = acc[h].astype(jnp.bfloat16)
            u_ref[h, width:, :] = jnp.broadcast_to(norm[h, 0:1, :], (PAD, width)).astype(
                jnp.bfloat16
            )


def memory_update(keys, values, heads, width):
    rows = keys.shape[0]
    block = 512
    return pl.pallas_call(
        functools.partial(update_kernel, heads, width),
        grid=(rows // block,),
        in_specs=[pl.BlockSpec((block, heads * width), lambda i: (i, 0))] * 2,
        out_specs=pl.BlockSpec((heads, width + PAD, width), lambda i: (0, 0, 0)),
        out_shape=jax.ShapeDtypeStruct((heads, width + PAD, width), jnp.bfloat16),
        scratch_shapes=[
            pltpu.VMEM((heads, width, width), jnp.float32),
            pltpu.VMEM((heads, 8, width), jnp.float32),
        ],
        compiler_params=pltpu.CompilerParams(vmem_limit_bytes=60 << 20),
        cost_estimate=pl.CostEstimate(
            flops=2 * rows * heads * width * width,
            transcendentals=rows * heads * width,
            bytes_accessed=4 * rows * heads * width,
        ),
    )(keys, values)


def attention_kernel(heads, width, first, tile, gate_ref, q_ref, k_ref, v_ref, m_ref, *rest):
    o_ref = rest[-1]
    rows = q_ref.shape[0]
    factor = LOG2E * width ** (-0.5)
    blocks = (first + rows) // tile
    row = lax.broadcasted_iota(jnp.int32, (rows, tile), 0)
    col = lax.broadcasted_iota(jnp.int32, (rows, tile), 1)
    for h in range(heads):
        cols = slice(h * width, (h + 1) * width)
        q = q_ref[:, cols]
        scores = []
        for j in range(blocks):
            s = dot(q, k_ref[j * tile : (j + 1) * tile, cols], ((1,), (1,))) * factor
            if (j + 1) * tile > first + 1:
                s = jnp.where(col + j * tile <= row + first, s, -jnp.inf)
            scores.append(s)
        top = scores[0]
        for s in scores[1:]:
            top = jnp.maximum(top, s)
        top = jnp.max(top, axis=1, keepdims=True)
        total = jnp.zeros((rows, 1), jnp.float32)
        mixed = jnp.zeros((rows, width), jnp.float32)
        for j in range(blocks):
            p = jnp.exp2(scores[j] - top)
            total += jnp.sum(p, axis=1, keepdims=True)
            mixed += dot(p.astype(jnp.bfloat16), v_ref[j * tile : (j + 1) * tile, cols], ((1,), (0,)))
        lifted = lift(q.astype(jnp.float32)).astype(jnp.bfloat16)
        numerator = dot(lifted, m_ref[h, :width, :], ((1,), (0,)))
        norm = m_ref[h, width : width + 1, :].astype(jnp.float32)
        denominator = jnp.sum(lifted.astype(jnp.float32) * norm, axis=1, keepdims=True) + 1.0
        blend = 1.0 / (1.0 + jnp.exp(jnp.full((1, 1), -gate_ref[h], jnp.float32)))
        mixed = mixed * ((1.0 - blend) / total) + numerator * (blend / denominator)
        mean = jnp.mean(mixed * mixed, axis=1, keepdims=True)
        o_ref[:, cols] = (mixed * lax.rsqrt(mean + EPS)).astype(jnp.bfloat16)


def attention_piece(q, k, v, memory, gate, out, heads, width, first, rows):
    total, lanes = q.shape
    span = first + rows
    row_spec = pl.BlockSpec((rows, lanes), lambda i: (first // rows, 0))
    span_spec = pl.BlockSpec((span, lanes), lambda i: (0, 0))
    args = [gate, q, k, v, memory]
    specs = [
        pl.BlockSpec(memory_space=pltpu.SMEM),
        row_spec,
        span_spec,
        span_spec,
        pl.BlockSpec(memory.shape, lambda i: (0, 0, 0)),
    ]
    aliases = {}
    if out is not None:
        args.append(out)
        specs.append(pl.BlockSpec(memory_space=pl.ANY))
        aliases = {5: 0}
    return pl.pallas_call(
        functools.partial(attention_kernel, heads, width, first, 512),
        grid=(1,),
        in_specs=specs,
        out_specs=row_spec,
        out_shape=jax.ShapeDtypeStruct((total, lanes), jnp.bfloat16),
        input_output_aliases=aliases,
        compiler_params=pltpu.CompilerParams(vmem_limit_bytes=40 << 20),
        cost_estimate=pl.CostEstimate(
            flops=4 * rows * span * lanes,
            transcendentals=rows * span * heads,
            bytes_accessed=2 * lanes * (2 * rows + 2 * span),
        ),
    )(*args)


def step_kernel(heads, width, parts, *refs):
    state_refs, (wq_ref, wo_ref, m_ref), out_refs = refs[:parts], refs[parts : parts + 3], refs[parts + 3 :]
    size = state_refs[0].shape[0]
    state = jnp.concatenate([r[...] for r in state_refs], axis=0)
    reads = []
    for h in range(heads):
        cols = slice(h * width, (h + 1) * width)
        lifted = lift(dot(state, wq_ref[:, cols], ((1,), (0,)))).astype(jnp.bfloat16)
        numerator = dot(lifted, m_ref[h, :width, :], ((1,), (0,)))
        norm = m_ref[h, width : width + 1, :].astype(jnp.float32)
        denominator = jnp.sum(lifted.astype(jnp.float32) * norm, axis=1, keepdims=True) + 1.0
        read = numerator / denominator
        mean = jnp.mean(read * read, axis=1, keepdims=True)
        reads.append((read * lax.rsqrt(mean + EPS)).astype(jnp.bfloat16))
    partial = dot(jnp.concatenate(reads, axis=1), wo_ref[...], ((1,), (0,)))
    for j in range(parts):
        out_refs[j][...] = partial[j * size : (j + 1) * size].astype(jnp.bfloat16)


def summary_step(pieces, wq, wo, memory, heads, width):
    parts = len(pieces)
    shape = pieces[0].shape
    rows = parts * shape[0]
    return pl.pallas_call(
        functools.partial(step_kernel, heads, width, parts),
        in_specs=[pl.BlockSpec(memory_space=pltpu.VMEM)] * (parts + 3),
        out_specs=[pl.BlockSpec(memory_space=pltpu.VMEM)] * parts,
        out_shape=[jax.ShapeDtypeStruct(shape, jnp.bfloat16)] * parts,
        compiler_params=pltpu.CompilerParams(vmem_limit_bytes=16 << 20),
        cost_estimate=pl.CostEstimate(
            flops=2 * rows * (wq.size + wo.size),
            transcendentals=rows * heads * width,
            bytes_accessed=2 * (wq.size + wo.size) + 4 * rows * shape[1],
        ),
    )(*pieces, wq, wo, memory)


def partner(x, axis, flip):
    return lax.ppermute(x, axis, [(i, i ^ flip) for i in range(lax.axis_size(axis))])


def scan_memory(own, decay, axis):
    count, me = lax.axis_size(axis), lax.axis_index(axis)
    shape = own.shape
    total, prior = own, jnp.zeros_like(own)
    order = jnp.arange(count)
    level = 1
    while level < count:
        mine = (order // level) == (me // level)
        theirs = (order // level) == ((me ^ level) // level)

        def product(mask):
            return jnp.prod(jnp.where(mask[:, None], decay, 1.0), axis=0)[:, None, None]

        got = partner(total, axis, level).astype(jnp.float32)
        later = (me & level) != 0
        before_me = product(mine & (order < me))
        kept = total.astype(jnp.float32)
        prior = jnp.where(later, before_me * got + prior.astype(jnp.float32), prior.astype(jnp.float32)).astype(
            jnp.bfloat16
        )
        total = jnp.where(later, product(mine) * got + kept, product(theirs) * kept + got).astype(jnp.bfloat16)
        level *= 2
    return total, prior


def on_device(queries, keys, values, decay, gate, summary, wq_sum, wo_sum):
    heads = gate.shape[0]
    width = queries.shape[1] // heads
    parts, me = lax.axis_size("sub"), lax.axis_index("sub")

    own = memory_update(keys, values, heads, width)
    final, prior = scan_memory(own, decay, "seq")

    piece_rows = summary.shape[0] // parts
    pieces = [
        lax.dynamic_slice_in_dim(summary, (me ^ j) * piece_rows, piece_rows, 0) for j in range(parts)
    ]
    attended = None
    chunk = 512
    waiting = list(range(0, SEG, chunk))

    def fill(after, attended):
        if not waiting:
            return attended
        tied, _ = lax.optimization_barrier((gate, after))
        return attention_piece(queries, keys, values, prior, tied, attended, heads, width, waiting.pop(0), chunk)

    for step in range(STEPS):
        partial = summary_step(pieces, wq_sum, wo_sum, final, heads, width)
        got = [partner(partial[j], "sub", j) for j in range(parts - 1, 0, -1)]
        attended = fill(partial[0], attended)
        got, attended = lax.optimization_barrier((got, attended))
        new = pieces[0].astype(jnp.float32) + partial[0].astype(jnp.float32)
        for g in got:
            new = new + g.astype(jnp.float32)
        new = new.astype(jnp.bfloat16)
        got = [partner(new, "sub", j) for j in range(parts - 1, 0, -1)][::-1]
        attended = fill(new, attended)
        got, attended = lax.optimization_barrier((got, attended))
        pieces = [new] + got
    out = jnp.zeros_like(summary)
    for j in range(parts):
        out = lax.dynamic_update_slice_in_dim(out, pieces[j], (me ^ j) * piece_rows, 0)
    return (attended, out)


def solution(mesh):
    placed = (
        P(("book", "seq"), "sub"),
        P(("book", "seq"), "sub"),
        P(("book", "seq"), "sub"),
        P("book", "sub"),
        P("sub"),
        P(("book", "seq"), None),
        P(None, "sub"),
        P("sub", None),
    )
    return jax.shard_map(
        on_device,
        mesh=mesh,
        in_specs=placed,
        out_specs=(P(("book", "seq"), "sub"), P(("book", "seq"), None)),
        check_vma=False,
    )
```

```python
import functools

import jax
import jax.numpy as jnp
from jax import lax
from jax.experimental import pallas as pl
from jax.experimental.pallas import tpu as pltpu
from jax.sharding import PartitionSpec as P

SEG = 2048
STEPS = 4
EPS = 1e-06
LOG2E = 1.4426950408889634
PAD = 16
QUERY_STAGES = (("book", 1), ("seq", 2), ("seq", 1))
OUTPUT_STAGES = (("seq", 2), ("book", 1), ("seq", 1))


def lift(x):
    return jnp.where(x > 0.0, x + 1.0, jnp.exp(jnp.minimum(x, 0.0)))


def dot(a, b, dims):
    return lax.dot_general(a, b, (dims, ((), ())), preferred_element_type=jnp.float32)


def update_kernel(heads, width, k_ref, v_ref, u_ref, acc, norm):
    step = pl.program_id(0)

    @pl.when(step == 0)
    def _():
        acc[...] = jnp.zeros_like(acc)
        norm[...] = jnp.zeros_like(norm)

    for h in range(heads):
        cols = slice(h * width, (h + 1) * width)
        lifted = lift(k_ref[:, cols].astype(jnp.float32))
        norm[h, 0:1, :] += jnp.sum(lifted, axis=0, keepdims=True)
        acc[h] += dot(lifted.astype(jnp.bfloat16), v_ref[:, cols], ((0,), (0,)))

    @pl.when(step == pl.num_programs(0) - 1)
    def _():
        for h in range(heads):
            u_ref[h, :width, :] = acc[h].astype(jnp.bfloat16)
            u_ref[h, width:, :] = jnp.broadcast_to(norm[h, 0:1, :], (PAD, width)).astype(
                jnp.bfloat16
            )


def memory_update(keys, values, heads, width):
    rows = keys.shape[0]
    block = 512
    return pl.pallas_call(
        functools.partial(update_kernel, heads, width),
        grid=(rows // block,),
        in_specs=[pl.BlockSpec((block, heads * width), lambda i: (i, 0))] * 2,
        out_specs=pl.BlockSpec((heads, width + PAD, width), lambda i: (0, 0, 0)),
        out_shape=jax.ShapeDtypeStruct((heads, width + PAD, width), jnp.bfloat16),
        scratch_shapes=[
            pltpu.VMEM((heads, width, width), jnp.float32),
            pltpu.VMEM((heads, 8, width), jnp.float32),
        ],
        compiler_params=pltpu.CompilerParams(vmem_limit_bytes=60 << 20),
        cost_estimate=pl.CostEstimate(
            flops=2 * rows * heads * width * width,
            transcendentals=rows * heads * width,
            bytes_accessed=4 * rows * heads * width,
        ),
    )(keys, values)


def attention_kernel(heads, width, first, tile, gate_ref, q_ref, k_ref, v_ref, m_ref, *rest):
    o_ref = rest[-1]
    rows = q_ref.shape[0]
    factor = LOG2E * width ** (-0.5)
    blocks = (first + rows) // tile
    row = lax.broadcasted_iota(jnp.int32, (rows, tile), 0)
    col = lax.broadcasted_iota(jnp.int32, (rows, tile), 1)
    for h in range(heads):
        cols = slice(h * width, (h + 1) * width)
        q = q_ref[:, cols]
        scores = []
        for j in range(blocks):
            s = dot(q, k_ref[j * tile : (j + 1) * tile, cols], ((1,), (1,))) * factor
            if (j + 1) * tile > first + 1:
                s = jnp.where(col + j * tile <= row + first, s, -jnp.inf)
            scores.append(s)
        top = scores[0]
        for s in scores[1:]:
            top = jnp.maximum(top, s)
        top = jnp.max(top, axis=1, keepdims=True)
        total = jnp.zeros((rows, 1), jnp.float32)
        mixed = jnp.zeros((rows, width), jnp.float32)
        for j in range(blocks):
            p = jnp.exp2(scores[j] - top)
            total += jnp.sum(p, axis=1, keepdims=True)
            mixed += dot(p.astype(jnp.bfloat16), v_ref[j * tile : (j + 1) * tile, cols], ((1,), (0,)))
        lifted = lift(q.astype(jnp.float32)).astype(jnp.bfloat16)
        numerator = dot(lifted, m_ref[h, :width, :], ((1,), (0,)))
        norm = m_ref[h, width : width + 1, :].astype(jnp.float32)
        denominator = jnp.sum(lifted.astype(jnp.float32) * norm, axis=1, keepdims=True) + 1.0
        blend = 1.0 / (1.0 + jnp.exp(jnp.full((1, 1), -gate_ref[h], jnp.float32)))
        mixed = mixed * ((1.0 - blend) / total) + numerator * (blend / denominator)
        mean = jnp.mean(mixed * mixed, axis=1, keepdims=True)
        o_ref[:, cols] = (mixed * lax.rsqrt(mean + EPS)).astype(jnp.bfloat16)


def attention_piece(q, k, v, memory, gate, out, heads, width, first, rows):
    total, lanes = q.shape
    span = first + rows
    row_spec = pl.BlockSpec((rows, lanes), lambda i: (first // rows, 0))
    span_spec = pl.BlockSpec((span, lanes), lambda i: (0, 0))
    args = [gate, q, k, v, memory]
    specs = [
        pl.BlockSpec(memory_space=pltpu.SMEM),
        row_spec,
        span_spec,
        span_spec,
        pl.BlockSpec(memory.shape, lambda i: (0, 0, 0)),
    ]
    aliases = {}
    if out is not None:
        args.append(out)
        specs.append(pl.BlockSpec(memory_space=pl.ANY))
        aliases = {5: 0}
    return pl.pallas_call(
        functools.partial(attention_kernel, heads, width, first, 512),
        grid=(1,),
        in_specs=specs,
        out_specs=row_spec,
        out_shape=jax.ShapeDtypeStruct((total, lanes), jnp.bfloat16),
        input_output_aliases=aliases,
        compiler_params=pltpu.CompilerParams(vmem_limit_bytes=40 << 20),
        cost_estimate=pl.CostEstimate(
            flops=4 * rows * span * lanes,
            transcendentals=rows * span * heads,
            bytes_accessed=2 * lanes * (2 * rows + 2 * span),
        ),
    )(*args)


def step_kernel(heads, width, parts, *refs):
    state_refs, (wq_ref, wo_ref, m_ref), out_refs = refs[:parts], refs[parts : parts + 3], refs[parts + 3 :]
    size = state_refs[0].shape[0]
    state = jnp.concatenate([r[...] for r in state_refs], axis=0)
    reads = []
    for h in range(heads):
        cols = slice(h * width, (h + 1) * width)
        lifted = lift(dot(state, wq_ref[:, cols], ((1,), (0,)))).astype(jnp.bfloat16)
        numerator = dot(lifted, m_ref[h, :width, :], ((1,), (0,)))
        norm = m_ref[h, width : width + 1, :].astype(jnp.float32)
        denominator = jnp.sum(lifted.astype(jnp.float32) * norm, axis=1, keepdims=True) + 1.0
        read = numerator / denominator
        mean = jnp.mean(read * read, axis=1, keepdims=True)
        reads.append((read * lax.rsqrt(mean + EPS)).astype(jnp.bfloat16))
    partial = dot(jnp.concatenate(reads, axis=1), wo_ref[...], ((1,), (0,)))
    for j in range(parts):
        out_refs[j][...] = partial[j * size : (j + 1) * size].astype(jnp.bfloat16)


def summary_step(pieces, wq, wo, memory, heads, width):
    parts = len(pieces)
    shape = pieces[0].shape
    rows = parts * shape[0]
    return pl.pallas_call(
        functools.partial(step_kernel, heads, width, parts),
        in_specs=[pl.BlockSpec(memory_space=pltpu.VMEM)] * (parts + 3),
        out_specs=[pl.BlockSpec(memory_space=pltpu.VMEM)] * parts,
        out_shape=[jax.ShapeDtypeStruct(shape, jnp.bfloat16)] * parts,
        compiler_params=pltpu.CompilerParams(vmem_limit_bytes=16 << 20),
        cost_estimate=pl.CostEstimate(
            flops=2 * rows * (wq.size + wo.size),
            transcendentals=rows * heads * width,
            bytes_accessed=2 * (wq.size + wo.size) + 4 * rows * shape[1],
        ),
    )(*pieces, wq, wo, memory)


def wide_kernel(heads, width, slices, place_ref, state_ref, wq_ref, wo_ref, m_ref, qa_ref, qb_ref, oa_ref, ob_ref, mx_ref, out_ref, acc):
    group = heads * width
    depth = state_ref.shape[1] // slices

    def read(lifted, memory_ref, h):
        numerator = dot(lifted, memory_ref[h, :width, :], ((1,), (0,)))
        norm = memory_ref[h, width : width + 1, :].astype(jnp.float32)
        denominator = jnp.sum(lifted.astype(jnp.float32) * norm, axis=1, keepdims=True) + 1.0
        value = numerator / denominator
        mean = jnp.mean(value * value, axis=1, keepdims=True)
        return (value * lax.rsqrt(mean + EPS)).astype(jnp.bfloat16)

    def reads(query, memory_ref):
        lifted = lift(query).astype(jnp.bfloat16)
        return jnp.concatenate(
            [read(lifted[:, h * width : (h + 1) * width], memory_ref, h) for h in range(heads)], axis=1
        )

    own = reads(dot(state_ref[...], wq_ref[...], ((1,), (0,))), m_ref)
    query = jnp.zeros((state_ref.shape[0], group), jnp.float32)
    half = slices // 2
    for j in range(slices):
        block = qa_ref[j] if j < half else qb_ref[j - half]
        at = pl.multiple_of((place_ref[0] ^ j) * depth, depth)
        query += dot(state_ref[:, pl.ds(at, depth)], block, ((1,), (0,)))
    other = reads(query, mx_ref)
    acc[...] = dot(own, wo_ref[...], ((1,), (0,)))
    for j in range(slices):
        block = oa_ref[j] if j < half else ob_ref[j - half]
        at = pl.multiple_of((place_ref[1] ^ j) * depth, depth)
        acc[:, pl.ds(at, depth)] += dot(other, block, ((1,), (0,)))
    out_ref[...] = acc[...].astype(jnp.bfloat16)


def wide_step(place, state, wq, wo, memory, query_side, output_side, other_memory, heads, width):
    rows, lanes = state.shape
    slices = query_side[0].shape[0] * 2
    vmem = pl.BlockSpec(memory_space=pltpu.VMEM)
    return pl.pallas_call(
        functools.partial(wide_kernel, heads, width, slices),
        in_specs=[pl.BlockSpec(memory_space=pltpu.SMEM)] + [vmem] * 9,
        out_specs=vmem,
        out_shape=jax.ShapeDtypeStruct((rows, lanes), jnp.bfloat16),
        scratch_shapes=[pltpu.VMEM((rows, lanes), jnp.float32)],
        compiler_params=pltpu.CompilerParams(vmem_limit_bytes=24 << 20),
        cost_estimate=pl.CostEstimate(
            flops=4 * rows * (wq.size + wo.size),
            transcendentals=2 * rows * heads * width,
            bytes_accessed=4 * (wq.size + wo.size) + 4 * rows * lanes,
        ),
    )(place, state, wq, wo, memory, *query_side, *output_side, other_memory)


def partner(x, axis, flip):
    return lax.ppermute(x, axis, [(i, i ^ flip) for i in range(lax.axis_size(axis))])


def scan_memory(own, decay, axis):
    count, me = lax.axis_size(axis), lax.axis_index(axis)
    shape = own.shape
    total, prior = own, jnp.zeros_like(own)
    order = jnp.arange(count)
    level = 1
    while level < count:
        mine = (order // level) == (me // level)
        theirs = (order // level) == ((me ^ level) // level)

        def product(mask):
            return jnp.prod(jnp.where(mask[:, None], decay, 1.0), axis=0)[:, None, None]

        got = partner(total, axis, level).astype(jnp.float32)
        later = (me & level) != 0
        before_me = product(mine & (order < me))
        kept = total.astype(jnp.float32)
        prior = jnp.where(later, before_me * got + prior.astype(jnp.float32), prior.astype(jnp.float32)).astype(
            jnp.bfloat16
        )
        total = jnp.where(later, product(mine) * got + kept, product(theirs) * kept + got).astype(jnp.bfloat16)
        level *= 2
    return total, prior


def import_slice(block, stages):
    held = partner(block, "sub", 1)[None]
    for axis, flip in stages[:-1]:
        held = jnp.concatenate([held, partner(held, axis, flip)], axis=0)
    return held, partner(held, *stages[-1])


def slice_index(stages):
    place = jnp.int32(0)
    for k, (axis, flip) in enumerate(stages):
        place += jnp.where((lax.axis_index(axis) & flip) != 0, 1 << k, 0).astype(jnp.int32)
    return place


def tree_sum(terms):
    while len(terms) > 1:
        terms = [terms[i] + terms[i + 1] for i in range(0, len(terms), 2)]
    return terms[0]


def wide_sum(terms):
    return tree_sum([t.astype(jnp.float32) for t in terms])


def on_device(queries, keys, values, decay, gate, summary, wq_sum, wo_sum):
    heads = gate.shape[0]
    width = queries.shape[1] // heads
    model = summary.shape[1]
    parts, me = lax.axis_size("sub"), lax.axis_index("sub")
    rows = summary.shape[0] // parts

    query_stages = QUERY_STAGES
    output_stages = OUTPUT_STAGES
    depth = model >> len(query_stages)
    query_place, output_place = slice_index(query_stages), slice_index(output_stages)
    place = jnp.stack([query_place, output_place])
    query_block = lax.dynamic_slice_in_dim(wq_sum, query_place * depth, depth, 0)
    output_block = lax.dynamic_slice_in_dim(wo_sum, output_place * depth, depth, 1)

    query_side = import_slice(query_block, query_stages)
    output_side = import_slice(output_block, output_stages)

    own = memory_update(keys, values, heads, width)
    final, prior = scan_memory(own, decay, "seq")
    other_final = partner(final, "sub", 1)

    flips = [(k << 1) | (k.bit_count() & 1) for k in range(parts // 2)]
    pieces = [lax.dynamic_slice_in_dim(summary, (me ^ j) * rows, rows, 0) for j in range(parts)]
    chunk = 512
    waiting = list(range(0, SEG, chunk))
    attended = None

    def fill(after, attended, count=1):
        for _ in range(count):
            if waiting:
                tied, _ = lax.optimization_barrier((gate, after))
                attended = attention_piece(
                    queries, keys, values, prior, tied, attended, heads, width, waiting.pop(0), chunk
                )
        return attended

    def swap(array, flip):
        order = [flips.index(f ^ flip) for f in flips]
        return jnp.concatenate([array[k * rows : (k + 1) * rows] for k in order], axis=0)

    state = jnp.concatenate([pieces[f] for f in flips], axis=0)
    partial = summary_step(pieces, wq_sum, wo_sum, final, heads, width)
    terms = [None] * parts
    mine = jnp.concatenate([partial[f] for f in flips], axis=0)
    for j in range(parts - 1, 0, -1):
        sent = jnp.concatenate([partial[j ^ f] for f in flips], axis=0)
        terms[j] = partner(sent, "sub", j)
    attended = fill(partial[0], attended, 2)
    terms[0] = mine
    terms, attended = lax.optimization_barrier((terms, attended))
    ordered = [terms[f] for f in flips] + [terms[f ^ 1] for f in flips]
    state = (state.astype(jnp.float32) + wide_sum(ordered)).astype(jnp.bfloat16)

    for step in range(1, STEPS):
        partial = wide_step(
            place, state, wq_sum, wo_sum, final, query_side, output_side, other_final, heads, width
        )
        terms = [partial] + [partner(partial, "sub", f) for f in flips[1:]]
        attended = fill(partial, attended)
        terms, attended = lax.optimization_barrier((terms, attended))
        terms = [terms[0]] + [swap(t, f) for t, f in zip(terms[1:], flips[1:])]
        state = (state.astype(jnp.float32) + wide_sum(terms)).astype(jnp.bfloat16)

    other = partner(state, "sub", 1)
    out = jnp.zeros_like(summary)
    for k, f in enumerate(flips):
        out = lax.dynamic_update_slice_in_dim(out, state[k * rows : (k + 1) * rows], (me ^ f) * rows, 0)
        out = lax.dynamic_update_slice_in_dim(out, other[k * rows : (k + 1) * rows], (me ^ f ^ 1) * rows, 0)
    return (attended, out)


def solution(mesh):
    placed = (
        P(("book", "seq"), "sub"),
        P(("book", "seq"), "sub"),
        P(("book", "seq"), "sub"),
        P("book", "sub"),
        P("sub"),
        P(("book", "seq"), None),
        P(None, "sub"),
        P("sub", None),
    )
    return jax.shard_map(
        on_device,
        mesh=mesh,
        in_specs=placed,
        out_specs=(P(("book", "seq"), "sub"), P(("book", "seq"), None)),
        check_vma=False,
    )
```

```python
import functools

import jax
import jax.numpy as jnp
from jax import lax
from jax.experimental import pallas as pl
from jax.experimental.pallas import tpu as pltpu
from jax.sharding import PartitionSpec as P

SEG = 2048
STEPS = 4
EPS = 1e-06
LOG2E = 1.4426950408889634
PAD = 16
UPDATE_ROWS = 512
QUERY_STAGES = (("book", 1), ("seq", 1))
OUTPUT_STAGES = (("seq", 2), ("seq", 1))


def lift(x):
    return jnp.where(x > 0.0, x + 1.0, jnp.exp(jnp.minimum(x, 0.0)))


def dot(a, b, dims):
    return lax.dot_general(a, b, (dims, ((), ())), preferred_element_type=jnp.float32)


def update_kernel(
    heads, width, block, depth, place_ref, k_hbm, v_hbm, wq_hbm, wo_hbm, u_ref, query_ref, output_ref, k_ref, v_ref, acc, norm, sems
):
    count = k_hbm.shape[0] // block
    at = [pl.multiple_of(place_ref[i] * depth, depth) for i in range(2)]
    slices = [
        pltpu.make_async_copy(wq_hbm.at[pl.ds(at[0], depth), :], query_ref, sems.at[2 * count]),
        pltpu.make_async_copy(wo_hbm.at[:, pl.ds(at[1], depth)], output_ref, sems.at[2 * count + 1]),
    ]
    copies = []
    for i in range(count):
        part = pl.ds(i * block, block)
        pair = (
            pltpu.make_async_copy(k_hbm.at[part], k_ref.at[part], sems.at[2 * i]),
            pltpu.make_async_copy(v_hbm.at[part], v_ref.at[part], sems.at[2 * i + 1]),
        )
        pair[0].start()
        pair[1].start()
        copies.append(pair)
    for copy in slices:
        copy.start()
    for i in range(count):
        part = slice(i * block, (i + 1) * block)
        copies[i][0].wait()
        copies[i][1].wait()
        for h in range(heads):
            cols = slice(h * width, (h + 1) * width)
            lifted = lift(k_ref[part, cols].astype(jnp.float32))
            total = jnp.sum(lifted, axis=0, keepdims=True)
            product = dot(lifted.astype(jnp.bfloat16), v_ref[part, cols], ((0,), (0,)))
            if i == 0:
                norm[h, 0:1, :] = total
                acc[h] = product
            else:
                norm[h, 0:1, :] += total
                acc[h] += product
    for h in range(heads):
        u_ref[h, :width, :] = acc[h].astype(jnp.bfloat16)
        u_ref[h, width:, :] = jnp.broadcast_to(norm[h, 0:1, :], (PAD, width)).astype(jnp.bfloat16)
    for copy in slices:
        copy.wait()


def memory_update(place, keys, values, wq, wo, depth, heads, width):
    rows, lanes = keys.shape
    count = rows // UPDATE_ROWS
    hbm = pl.BlockSpec(memory_space=pltpu.HBM)
    return pl.pallas_call(
        functools.partial(update_kernel, heads, width, UPDATE_ROWS, depth),
        in_specs=[pl.BlockSpec(memory_space=pltpu.SMEM)] + [hbm] * 4,
        out_specs=[pl.BlockSpec(memory_space=pltpu.VMEM)] * 3,
        out_shape=[
            jax.ShapeDtypeStruct((heads, width + PAD, width), jnp.bfloat16),
            jax.ShapeDtypeStruct((depth, wq.shape[1]), wq.dtype),
            jax.ShapeDtypeStruct((wo.shape[0], depth), wo.dtype),
        ],
        scratch_shapes=[
            pltpu.VMEM((rows, lanes), jnp.bfloat16),
            pltpu.VMEM((rows, lanes), jnp.bfloat16),
            pltpu.VMEM((heads, width, width), jnp.float32),
            pltpu.VMEM((heads, 8, width), jnp.float32),
            pltpu.SemaphoreType.DMA((2 * count + 2,)),
        ],
        compiler_params=pltpu.CompilerParams(vmem_limit_bytes=60 << 20),
        cost_estimate=pl.CostEstimate(
            flops=2 * rows * heads * width * width,
            transcendentals=rows * heads * width,
            bytes_accessed=4 * rows * heads * width,
        ),
    )(place, keys, values, wq, wo)


def lifted_query(state, wq):
    rows, depth = state.shape
    block = depth // 4
    return pl.pallas_call(
        query_kernel,
        grid=(4,),
        in_specs=[pl.BlockSpec((rows, block), lambda i: (0, i)), pl.BlockSpec((block, wq.shape[1]), lambda i: (i, 0))],
        out_specs=pl.BlockSpec((rows, wq.shape[1]), lambda i: (0, 0)),
        out_shape=jax.ShapeDtypeStruct((rows, wq.shape[1]), jnp.bfloat16),
        scratch_shapes=[pltpu.VMEM((rows, wq.shape[1]), jnp.float32)],
        compiler_params=pltpu.CompilerParams(vmem_limit_bytes=8 << 20),
        cost_estimate=pl.CostEstimate(
            flops=2 * rows * wq.size, transcendentals=rows * wq.shape[1], bytes_accessed=2 * wq.size
        ),
    )(state, wq)


def query_kernel(s_ref, w_ref, o_ref, acc):
    product = dot(s_ref[...], w_ref[...], ((1,), (0,)))

    @pl.when(pl.program_id(0) == 0)
    def _():
        acc[...] = product

    @pl.when(pl.program_id(0) != 0)
    def _():
        acc[...] += product

    @pl.when(pl.program_id(0) == pl.num_programs(0) - 1)
    def _():
        o_ref[...] = lift(acc[...]).astype(jnp.bfloat16)


def attention_kernel(heads, head, width, first, rows, tile, gate_ref, q_ref, k_ref, v_ref, m_ref, *rest):
    o_ref = rest[-1]
    at = first if q_ref.shape[0] > rows else 0
    factor = LOG2E * width ** (-0.5)
    blocks = (first + rows) // tile
    row = lax.broadcasted_iota(jnp.int32, (rows, tile), 0)
    col = lax.broadcasted_iota(jnp.int32, (rows, tile), 1)
    for h in range(head, head + heads):
        cols = slice(h * width, (h + 1) * width)
        q = q_ref[at : at + rows, cols]
        scores = []
        for j in range(blocks):
            s = dot(q, k_ref[j * tile : (j + 1) * tile, cols], ((1,), (1,))) * factor
            if (j + 1) * tile > first + 1:
                s = jnp.where(col + j * tile <= row + first, s, -jnp.inf)
            scores.append(s)
        top = scores[0]
        for s in scores[1:]:
            top = jnp.maximum(top, s)
        top = jnp.max(top, axis=1, keepdims=True)
        total = jnp.zeros((rows, 1), jnp.float32)
        mixed = jnp.zeros((rows, width), jnp.float32)
        for j in range(blocks):
            p = jnp.exp2(scores[j] - top)
            total += jnp.sum(p, axis=1, keepdims=True)
            mixed += dot(p.astype(jnp.bfloat16), v_ref[j * tile : (j + 1) * tile, cols], ((1,), (0,)))
        lifted = lift(q.astype(jnp.float32)).astype(jnp.bfloat16)
        numerator = dot(lifted, m_ref[h, :width, :], ((1,), (0,)))
        norm = m_ref[h, width : width + 1, :].astype(jnp.float32)
        denominator = jnp.sum(lifted.astype(jnp.float32) * norm, axis=1, keepdims=True) + 1.0
        blend = 1.0 / (1.0 + jnp.exp(jnp.full((1, 1), -gate_ref[h], jnp.float32)))
        mixed = mixed * ((1.0 - blend) / total) + numerator * (blend / denominator)
        mean = jnp.mean(mixed * mixed, axis=1, keepdims=True)
        out = slice((h - head) * width, (h - head + 1) * width)
        o_ref[:, out] = (mixed * lax.rsqrt(mean + EPS)).astype(jnp.bfloat16)


def attention_piece(q, k, v, memory, gate, out, width, first, rows, head, heads):
    lanes = heads * width
    span = first + rows
    vmem = pl.BlockSpec(memory_space=pltpu.VMEM)
    args = [gate, q, k, v, memory]
    specs = [pl.BlockSpec(memory_space=pltpu.SMEM)] + [vmem] * 4
    aliases = {}
    if True:
        specs[1] = pl.BlockSpec((rows, q.shape[1]), lambda i: (first // rows, 0))
        specs[2] = specs[3] = pl.BlockSpec((span, q.shape[1]), lambda i: (0, 0))
    if out is not None:
        args.append(out)
        specs.append(pl.BlockSpec(memory_space=pl.ANY))
        aliases = {5: 0}
    return pl.pallas_call(
        functools.partial(attention_kernel, heads, head, width, first, rows, 512),
        grid=(1,),
        in_specs=specs,
        out_specs=pl.BlockSpec((rows, lanes), lambda i: (first // rows, head // heads)),
        out_shape=jax.ShapeDtypeStruct(q.shape, jnp.bfloat16),
        input_output_aliases=aliases,
        compiler_params=pltpu.CompilerParams(vmem_limit_bytes=24 << 20),
        cost_estimate=pl.CostEstimate(
            flops=4 * rows * span * lanes,
            transcendentals=rows * span * heads,
            bytes_accessed=2 * lanes * (2 * rows + 2 * span),
        ),
    )(*args)


def read_memory(lifted, memory_ref, h, width):
    numerator = dot(lifted, memory_ref[h, :width, :], ((1,), (0,)))
    norm = memory_ref[h, width : width + 1, :].astype(jnp.float32)
    denominator = jnp.sum(lifted.astype(jnp.float32) * norm, axis=1, keepdims=True) + 1.0
    value = numerator / denominator
    mean = jnp.mean(value * value, axis=1, keepdims=True)
    return (value * lax.rsqrt(mean + EPS)).astype(jnp.bfloat16)


def read_heads(lifted, memory_ref, heads, width):
    return jnp.concatenate(
        [read_memory(lifted[:, h * width : (h + 1) * width], memory_ref, h, width) for h in range(heads)],
        axis=1,
    )


def first_kernel(heads, width, parts, flips, me_ref, state_ref, lifted_ref, wo_ref, m_ref, half_ref, kept_ref, sent_ref, acc):
    rows = state_ref.shape[0] // parts
    reads = read_heads(lifted_ref[...], m_ref, heads, width)
    acc[...] = dot(reads, wo_ref[...], ((1,), (0,)))
    for k, f in enumerate(flips):
        at = pl.multiple_of((me_ref[0] ^ f) * rows, rows)
        half_ref[k * rows : (k + 1) * rows, :] = state_ref[pl.ds(at, rows), :]
        for j, ref in enumerate((kept_ref, sent_ref)):
            at = pl.multiple_of((me_ref[0] ^ j ^ f) * rows, rows)
            ref[k * rows : (k + 1) * rows, :] = acc[pl.ds(at, rows), :].astype(jnp.bfloat16)


def first_step(me, state, lifted, wo, memory, heads, width, parts, flips):
    rows, lanes = state.shape
    vmem = pl.BlockSpec(memory_space=pltpu.VMEM)
    shape = jax.ShapeDtypeStruct((rows // parts * len(flips), lanes), jnp.bfloat16)
    return pl.pallas_call(
        functools.partial(first_kernel, heads, width, parts, flips),
        in_specs=[pl.BlockSpec(memory_space=pltpu.SMEM)] + [vmem] * 4,
        out_specs=[vmem] * 3,
        out_shape=[shape] * 3,
        scratch_shapes=[pltpu.VMEM((rows, lanes), jnp.float32)],
        compiler_params=pltpu.CompilerParams(vmem_limit_bytes=12 << 20),
        cost_estimate=pl.CostEstimate(
            flops=2 * rows * wo.size,
            transcendentals=rows * heads * width,
            bytes_accessed=2 * wo.size + 4 * rows * lanes,
        ),
    )(me, state, lifted, wo, memory)


def wide_kernel(heads, width, slices, place_ref, state_ref, wq_ref, wo_ref, m_ref, mx_ref, *rest):
    query_refs, output_refs, (out_ref, acc) = rest[:slices], rest[slices : 2 * slices], rest[2 * slices :]
    group = heads * width
    depth = state_ref.shape[1] // slices

    own = read_heads(lift(dot(state_ref[...], wq_ref[...], ((1,), (0,)))).astype(jnp.bfloat16), m_ref, heads, width)
    query = jnp.zeros((state_ref.shape[0], group), jnp.float32)
    for j in range(slices):
        at = pl.multiple_of((place_ref[0] ^ j) * depth, depth)
        query += dot(state_ref[:, pl.ds(at, depth)], query_refs[j][...], ((1,), (0,)))
    other = read_heads(lift(query).astype(jnp.bfloat16), mx_ref, heads, width)
    acc[...] = dot(own, wo_ref[...], ((1,), (0,)))
    for j in range(slices):
        at = pl.multiple_of((place_ref[1] ^ j) * depth, depth)
        acc[:, pl.ds(at, depth)] += dot(other, output_refs[j][...], ((1,), (0,)))
    out_ref[...] = acc[...].astype(jnp.bfloat16)


def wide_step(place, state, wq, wo, memory, query_side, output_side, other_memory, heads, width):
    rows, lanes = state.shape
    slices = len(query_side)
    vmem = pl.BlockSpec(memory_space=pltpu.VMEM)
    return pl.pallas_call(
        functools.partial(wide_kernel, heads, width, slices),
        in_specs=[pl.BlockSpec(memory_space=pltpu.SMEM)] + [vmem] * (5 + 2 * slices),
        out_specs=vmem,
        out_shape=jax.ShapeDtypeStruct((rows, lanes), jnp.bfloat16),
        scratch_shapes=[pltpu.VMEM((rows, lanes), jnp.float32)],
        compiler_params=pltpu.CompilerParams(vmem_limit_bytes=24 << 20),
        cost_estimate=pl.CostEstimate(
            flops=4 * rows * (wq.size + wo.size),
            transcendentals=2 * rows * heads * width,
            bytes_accessed=4 * (wq.size + wo.size) + 4 * rows * lanes,
        ),
    )(place, state, wq, wo, memory, other_memory, *query_side, *output_side)


def partner(x, axis, flip):
    return lax.ppermute(x, axis, [(i, i ^ flip) for i in range(lax.axis_size(axis))])


def scan_memory(own, decay, axis, beside):
    count, me = lax.axis_size(axis), lax.axis_index(axis)
    shape = own.shape
    total, prior = own, jnp.zeros_like(own)
    order = jnp.arange(count)
    level = 1
    while level < count:
        mine = (order // level) == (me // level)
        theirs = (order // level) == ((me ^ level) // level)

        def product(mask):
            return jnp.prod(jnp.where(mask[:, None], decay, 1.0), axis=0)[:, None, None]

        got = partner(total, axis, level)
        if 2 * level >= count:
            extra = beside(total)
            got, extra = lax.optimization_barrier((got, extra))
        got = got.astype(jnp.float32)
        later = (me & level) != 0
        before_me = product(mine & (order < me))
        kept = total.astype(jnp.float32)
        prior = jnp.where(later, before_me * got + prior.astype(jnp.float32), prior.astype(jnp.float32)).astype(
            jnp.bfloat16
        )
        total = jnp.where(later, product(mine) * got + kept, product(theirs) * kept + got).astype(jnp.bfloat16)
        level *= 2
    return total, prior, extra


def widen(held, axis, flip):
    return held + [partner(piece, axis, flip) for piece in held]


def after(value, *events):
    return lax.optimization_barrier((value, events))[0]


def slice_index(stages):
    place = jnp.int32(0)
    for k, (axis, flip) in enumerate(stages):
        place += jnp.where((lax.axis_index(axis) & flip) != 0, 1 << k, 0).astype(jnp.int32)
    return place


def tree_sum(terms):
    while len(terms) > 1:
        terms = [terms[i] + terms[i + 1] for i in range(0, len(terms), 2)]
    return terms[0]


def wide_sum(terms):
    return tree_sum([t.astype(jnp.float32) for t in terms])


def on_device(queries, keys, values, decay, gate, summary, wq_sum, wo_sum):
    heads = gate.shape[0]
    width = queries.shape[1] // heads
    model = summary.shape[1]
    parts, me = lax.axis_size("sub"), lax.axis_index("sub")
    rows = summary.shape[0] // parts

    flips = tuple((k << 1) | (k.bit_count() & 1) for k in range(parts // 2))

    depth = model >> len(QUERY_STAGES)
    place = jnp.stack([slice_index(QUERY_STAGES), slice_index(OUTPUT_STAGES)])
    own, query_block, output_block = memory_update(
        place, keys, values, wq_sum, wo_sum, depth, heads, width
    )
    query_block = partner(query_block, "sub", 1)
    output_block = partner(output_block, "sub", 1)

    def scan():
        return scan_memory(
            own, decay, "seq", lambda event: lifted_query(after(summary, event), wq_sum)
        )

    def skip():
        empty = jnp.zeros((heads, width + PAD, width), jnp.bfloat16)
        return empty, empty, jnp.zeros((summary.shape[0], heads * width), jnp.bfloat16)

    final, prior, lifted = lax.cond(gate[0] == gate[0], scan, skip)

    chunk = 512

    def fill(event, attended, *places):
        for first, head, count in places:
            attended = attention_piece(
                queries, keys, values, prior, after(gate, event), attended, width, first, chunk, head, count
            )
        return attended

    def swap(array, flip):
        order = [flips.index(f ^ flip) for f in flips]
        return jnp.concatenate([array[k * rows : (k + 1) * rows] for k in order], axis=0)

    def exchange(partial):
        return [partial] + [partner(partial, "sub", f) for f in flips[1:]]

    def summed(state, terms):
        terms = [terms[0]] + [swap(t, f) for t, f in zip(terms[1:], flips[1:])]
        return (state.astype(jnp.float32) + wide_sum(terms)).astype(jnp.bfloat16)

    state, kept, sent = first_step(
        me.reshape(1), summary, lifted, wo_sum, final, heads, width, parts, flips
    )
    got = partner(sent, "sub", 1)
    query_other = partner(after(query_block, kept), *QUERY_STAGES[0])
    output_other = partner(after(output_block, kept), *OUTPUT_STAGES[0])
    other_final = partner(after(final, kept), "sub", 1)
    partial = wide_sum([kept, got]).astype(jnp.bfloat16)
    terms = exchange(partial)
    attended = fill(partial, None, (chunk, 0, heads))
    terms, attended, query_other, output_other, other_final = lax.optimization_barrier(
        (terms, attended, query_other, output_other, other_final)
    )
    query_side = widen([query_block, query_other], *QUERY_STAGES[1])
    output_side = widen([output_block, output_other], *OUTPUT_STAGES[1])
    attended = fill(terms[0], attended, (0, 0, heads))
    query_side, output_side, attended = lax.optimization_barrier((query_side, output_side, attended))
    state = summed(state, terms)

    last = [[(3 * chunk, 0, heads)], [(2 * chunk, 0, heads)], []]
    for step in range(1, STEPS):
        partial = wide_step(
            place, state, wq_sum, wo_sum, final, query_side, output_side, other_final, heads, width
        )
        terms = exchange(partial)
        attended = fill(partial, attended, *last[step - 1])
        terms, attended = lax.optimization_barrier((terms, attended))
        state = summed(state, terms)

    other = partner(state, "sub", 1)
    out = jnp.zeros_like(summary)
    for k, f in enumerate(flips):
        out = lax.dynamic_update_slice_in_dim(out, state[k * rows : (k + 1) * rows], (me ^ f) * rows, 0)
        out = lax.dynamic_update_slice_in_dim(out, other[k * rows : (k + 1) * rows], (me ^ f ^ 1) * rows, 0)
    return (attended, out)


def solution(mesh):
    placed = (
        P(("book", "seq"), "sub"),
        P(("book", "seq"), "sub"),
        P(("book", "seq"), "sub"),
        P("book", "sub"),
        P("sub"),
        P(("book", "seq"), None),
        P(None, "sub"),
        P("sub", None),
    )
    return jax.shard_map(
        on_device,
        mesh=mesh,
        in_specs=placed,
        out_specs=(P(("book", "seq"), "sub"), P(("book", "seq"), None)),
        check_vma=False,
    )
```

```python
import functools

import jax
import jax.numpy as jnp
from jax import lax
from jax.experimental import pallas as pl
from jax.experimental.pallas import tpu as pltpu
from jax.sharding import PartitionSpec as P

SEG = 2048
STEPS = 4
EPS = 1e-06
LOG2E = 1.4426950408889634
PAD = 16
UPDATE_ROWS = 512
QUERY_STAGES = (("book", 1), ("seq", 1))
OUTPUT_STAGES = (("seq", 2), ("seq", 1))


def lift(x):
    return jnp.where(x > 0.0, x + 1.0, jnp.exp(jnp.minimum(x, 0.0)))


def dot(a, b, dims):
    return lax.dot_general(a, b, (dims, ((), ())), preferred_element_type=jnp.float32)


def update_kernel(
    heads, width, block, depth, place_ref, k_hbm, v_hbm, wq_hbm, wo_hbm, u_ref, query_hbm, output_hbm,
    k_ref, v_ref, query_ref, output_ref, acc, norm, sems
):
    count = k_hbm.shape[0] // block
    at = [pl.multiple_of(place_ref[i] * depth, depth) for i in range(2)]
    slices = [
        pltpu.make_async_copy(wq_hbm.at[pl.ds(at[0], depth), :], query_ref, sems.at[2 * count]),
        pltpu.make_async_copy(wo_hbm.at[:, pl.ds(at[1], depth)], output_ref, sems.at[2 * count + 1]),
    ]
    backs = [
        pltpu.make_async_copy(query_ref, query_hbm, sems.at[2 * count + 2]),
        pltpu.make_async_copy(output_ref, output_hbm, sems.at[2 * count + 3]),
    ]
    for copy in slices:
        copy.start()
    copies = []
    for i in range(count):
        part = pl.ds(i * block, block)
        pair = (
            pltpu.make_async_copy(k_hbm.at[part], k_ref.at[part], sems.at[2 * i]),
            pltpu.make_async_copy(v_hbm.at[part], v_ref.at[part], sems.at[2 * i + 1]),
        )
        pair[0].start()
        pair[1].start()
        copies.append(pair)
    for i in range(count):
        part = slice(i * block, (i + 1) * block)
        copies[i][0].wait()
        copies[i][1].wait()
        if i == 0:
            for copy, back in zip(slices, backs):
                copy.wait()
                back.start()
        for h in range(heads):
            cols = slice(h * width, (h + 1) * width)
            lifted = lift(k_ref[part, cols].astype(jnp.float32))
            total = jnp.sum(lifted, axis=0, keepdims=True)
            product = dot(lifted.astype(jnp.bfloat16), v_ref[part, cols], ((0,), (0,)))
            if i == 0:
                norm[h, 0:1, :] = total
                acc[h] = product
            else:
                norm[h, 0:1, :] += total
                acc[h] += product
    for h in range(heads):
        u_ref[h, :width, :] = acc[h].astype(jnp.bfloat16)
        u_ref[h, width:, :] = jnp.broadcast_to(norm[h, 0:1, :], (PAD, width)).astype(jnp.bfloat16)
    for copy in backs:
        copy.wait()


def memory_update(place, keys, values, wq, wo, depth, heads, width):
    rows, lanes = keys.shape
    count = rows // UPDATE_ROWS
    hbm = pl.BlockSpec(memory_space=pltpu.HBM)
    return pl.pallas_call(
        functools.partial(update_kernel, heads, width, UPDATE_ROWS, depth),
        in_specs=[pl.BlockSpec(memory_space=pltpu.SMEM)] + [hbm] * 4,
        out_specs=[pl.BlockSpec(memory_space=pltpu.VMEM), hbm, hbm],
        out_shape=[
            jax.ShapeDtypeStruct((heads, width + PAD, width), jnp.bfloat16),
            jax.ShapeDtypeStruct((depth, wq.shape[1]), wq.dtype),
            jax.ShapeDtypeStruct((wo.shape[0], depth), wo.dtype),
        ],
        scratch_shapes=[
            pltpu.VMEM((rows, lanes), jnp.bfloat16),
            pltpu.VMEM((rows, lanes), jnp.bfloat16),
            pltpu.VMEM((depth, wq.shape[1]), wq.dtype),
            pltpu.VMEM((wo.shape[0], depth), wo.dtype),
            pltpu.VMEM((heads, width, width), jnp.float32),
            pltpu.VMEM((heads, 8, width), jnp.float32),
            pltpu.SemaphoreType.DMA((2 * count + 4,)),
        ],
        compiler_params=pltpu.CompilerParams(vmem_limit_bytes=60 << 20),
        cost_estimate=pl.CostEstimate(
            flops=2 * rows * heads * width * width,
            transcendentals=rows * heads * width,
            bytes_accessed=4 * rows * heads * width,
        ),
    )(place, keys, values, wq, wo)


def lifted_query(state, wq):
    rows, depth = state.shape
    block = depth // 4
    return pl.pallas_call(
        query_kernel,
        grid=(4,),
        in_specs=[pl.BlockSpec((rows, block), lambda i: (0, i)), pl.BlockSpec((block, wq.shape[1]), lambda i: (i, 0))],
        out_specs=pl.BlockSpec((rows, wq.shape[1]), lambda i: (0, 0)),
        out_shape=jax.ShapeDtypeStruct((rows, wq.shape[1]), jnp.bfloat16),
        scratch_shapes=[pltpu.VMEM((rows, wq.shape[1]), jnp.float32)],
        compiler_params=pltpu.CompilerParams(vmem_limit_bytes=8 << 20),
        cost_estimate=pl.CostEstimate(
            flops=2 * rows * wq.size, transcendentals=rows * wq.shape[1], bytes_accessed=2 * wq.size
        ),
    )(state, wq)


def query_kernel(s_ref, w_ref, o_ref, acc):
    product = dot(s_ref[...], w_ref[...], ((1,), (0,)))

    @pl.when(pl.program_id(0) == 0)
    def _():
        acc[...] = product

    @pl.when(pl.program_id(0) != 0)
    def _():
        acc[...] += product

    @pl.when(pl.program_id(0) == pl.num_programs(0) - 1)
    def _():
        o_ref[...] = lift(acc[...]).astype(jnp.bfloat16)


def attention_kernel(heads, head, width, first, rows, tile, gate_ref, q_ref, k_ref, v_ref, m_ref, *rest):
    o_ref = rest[-1]
    at = first if q_ref.shape[0] > rows else 0
    factor = LOG2E * width ** (-0.5)
    blocks = (first + rows) // tile
    row = lax.broadcasted_iota(jnp.int32, (rows, tile), 0)
    col = lax.broadcasted_iota(jnp.int32, (rows, tile), 1)
    for h in range(head, head + heads):
        cols = slice(h * width, (h + 1) * width)
        q = q_ref[at : at + rows, cols]
        scores = []
        for j in range(blocks):
            s = dot(q, k_ref[j * tile : (j + 1) * tile, cols], ((1,), (1,))) * factor
            if (j + 1) * tile > first + 1:
                s = jnp.where(col + j * tile <= row + first, s, -jnp.inf)
            scores.append(s)
        top = scores[0]
        for s in scores[1:]:
            top = jnp.maximum(top, s)
        top = jnp.max(top, axis=1, keepdims=True)
        total = jnp.zeros((rows, 1), jnp.float32)
        mixed = jnp.zeros((rows, width), jnp.float32)
        for j in range(blocks):
            p = jnp.exp2(scores[j] - top)
            total += jnp.sum(p, axis=1, keepdims=True)
            mixed += dot(p.astype(jnp.bfloat16), v_ref[j * tile : (j + 1) * tile, cols], ((1,), (0,)))
        lifted = lift(q.astype(jnp.float32)).astype(jnp.bfloat16)
        numerator = dot(lifted, m_ref[h, :width, :], ((1,), (0,)))
        norm = m_ref[h, width : width + 1, :].astype(jnp.float32)
        denominator = jnp.sum(lifted.astype(jnp.float32) * norm, axis=1, keepdims=True) + 1.0
        blend = 1.0 / (1.0 + jnp.exp(jnp.full((1, 1), -gate_ref[h], jnp.float32)))
        mixed = mixed * ((1.0 - blend) / total) + numerator * (blend / denominator)
        mean = jnp.mean(mixed * mixed, axis=1, keepdims=True)
        out = slice((h - head) * width, (h - head + 1) * width)
        o_ref[:, out] = (mixed * lax.rsqrt(mean + EPS)).astype(jnp.bfloat16)


def attention_piece(q, k, v, memory, gate, out, width, first, rows, head, heads):
    lanes = heads * width
    span = first + rows
    vmem = pl.BlockSpec(memory_space=pltpu.VMEM)
    args = [gate, q, k, v, memory]
    specs = [pl.BlockSpec(memory_space=pltpu.SMEM)] + [vmem] * 4
    aliases = {}
    if True:
        specs[1] = pl.BlockSpec((rows, q.shape[1]), lambda i: (first // rows, 0))
        specs[2] = specs[3] = pl.BlockSpec((span, q.shape[1]), lambda i: (0, 0))
    if out is not None:
        args.append(out)
        specs.append(pl.BlockSpec(memory_space=pl.ANY))
        aliases = {5: 0}
    return pl.pallas_call(
        functools.partial(attention_kernel, heads, head, width, first, rows, 512),
        grid=(1,),
        in_specs=specs,
        out_specs=pl.BlockSpec((rows, lanes), lambda i: (first // rows, head // heads)),
        out_shape=jax.ShapeDtypeStruct(q.shape, jnp.bfloat16),
        input_output_aliases=aliases,
        compiler_params=pltpu.CompilerParams(vmem_limit_bytes=24 << 20),
        cost_estimate=pl.CostEstimate(
            flops=4 * rows * span * lanes,
            transcendentals=rows * span * heads,
            bytes_accessed=2 * lanes * (2 * rows + 2 * span),
        ),
    )(*args)


def read_memory(lifted, memory_ref, h, width):
    numerator = dot(lifted, memory_ref[h, :width, :], ((1,), (0,)))
    norm = memory_ref[h, width : width + 1, :].astype(jnp.float32)
    denominator = jnp.sum(lifted.astype(jnp.float32) * norm, axis=1, keepdims=True) + 1.0
    value = numerator / denominator
    mean = jnp.mean(value * value, axis=1, keepdims=True)
    return (value * lax.rsqrt(mean + EPS)).astype(jnp.bfloat16)


def read_heads(lifted, memory_ref, heads, width):
    return jnp.concatenate(
        [read_memory(lifted[:, h * width : (h + 1) * width], memory_ref, h, width) for h in range(heads)],
        axis=1,
    )


def first_kernel(
    heads, width, flips, parts, me_ref, coef_ref, state_ref, lifted_ref, total_ref, got_ref, early_ref, wo_hbm,
    half_ref, kept_ref, sent_ref, final_ref, prior_ref, wo_ref, acc, sems
):
    rows = state_ref.shape[0] // parts
    copies = []
    for h in range(heads):
        part = pl.ds(h * width, width)
        copies.append(pltpu.make_async_copy(wo_hbm.at[part], wo_ref.at[part], sems.at[h]))
        copies[h].start()
    combine_kernel(heads, coef_ref, total_ref, got_ref, early_ref, final_ref, prior_ref)
    for h in range(heads):
        part = slice(h * width, (h + 1) * width)
        read = read_memory(lifted_ref[:, part], final_ref, h, width)
        copies[h].wait()
        product = dot(read, wo_ref[part, :], ((1,), (0,)))
        acc[...] = product if h == 0 else acc[...] + product
    for k, f in enumerate(flips):
        at = pl.multiple_of((me_ref[0] ^ f) * rows, rows)
        half_ref[k * rows : (k + 1) * rows, :] = state_ref[pl.ds(at, rows), :]
        for j, ref in enumerate((kept_ref, sent_ref)):
            at = pl.multiple_of((me_ref[0] ^ j ^ f) * rows, rows)
            ref[k * rows : (k + 1) * rows, :] = acc[pl.ds(at, rows), :].astype(jnp.bfloat16)


def first_step(me, coef, state, lifted, total, got, early, wo, heads, width, parts, flips):
    rows, lanes = state.shape
    vmem, smem = pl.BlockSpec(memory_space=pltpu.VMEM), pl.BlockSpec(memory_space=pltpu.SMEM)
    shape = jax.ShapeDtypeStruct((rows // parts * len(flips), lanes), jnp.bfloat16)
    memory = jax.ShapeDtypeStruct(total.shape, jnp.bfloat16)
    return pl.pallas_call(
        functools.partial(first_kernel, heads, width, flips, parts),
        in_specs=[smem, smem] + [vmem] * 5 + [pl.BlockSpec(memory_space=pltpu.HBM)],
        out_specs=[vmem] * 5,
        out_shape=[shape] * 3 + [memory] * 2,
        scratch_shapes=[
            pltpu.VMEM(wo.shape, wo.dtype),
            pltpu.VMEM((rows, lanes), jnp.float32),
            pltpu.SemaphoreType.DMA((heads,)),
        ],
        compiler_params=pltpu.CompilerParams(vmem_limit_bytes=16 << 20),
        cost_estimate=pl.CostEstimate(
            flops=2 * rows * wo.size,
            transcendentals=rows * heads * width,
            bytes_accessed=2 * wo.size + 4 * rows * lanes,
        ),
    )(me, coef, state, lifted, total, got, early, wo)


def wide_kernel(heads, width, slices, place_ref, state_ref, wq_ref, wo_ref, m_ref, mx_ref, *rest):
    query_refs, output_refs, (out_ref, acc) = rest[:slices], rest[slices : 2 * slices], rest[2 * slices :]
    group = heads * width
    depth = state_ref.shape[1] // slices

    own = read_heads(lift(dot(state_ref[...], wq_ref[...], ((1,), (0,)))).astype(jnp.bfloat16), m_ref, heads, width)
    query = jnp.zeros((state_ref.shape[0], group), jnp.float32)
    for j in range(slices):
        at = pl.multiple_of((place_ref[0] ^ j) * depth, depth)
        query += dot(state_ref[:, pl.ds(at, depth)], query_refs[j][...], ((1,), (0,)))
    other = read_heads(lift(query).astype(jnp.bfloat16), mx_ref, heads, width)
    acc[...] = dot(own, wo_ref[...], ((1,), (0,)))
    for j in range(slices):
        at = pl.multiple_of((place_ref[1] ^ j) * depth, depth)
        acc[:, pl.ds(at, depth)] += dot(other, output_refs[j][...], ((1,), (0,)))
    out_ref[...] = acc[...].astype(jnp.bfloat16)


def wide_step(place, state, wq, wo, memory, query_side, output_side, other_memory, heads, width):
    rows, lanes = state.shape
    slices = len(query_side)
    vmem = pl.BlockSpec(memory_space=pltpu.VMEM)
    return pl.pallas_call(
        functools.partial(wide_kernel, heads, width, slices),
        in_specs=[pl.BlockSpec(memory_space=pltpu.SMEM)] + [vmem] * (5 + 2 * slices),
        out_specs=vmem,
        out_shape=jax.ShapeDtypeStruct((rows, lanes), jnp.bfloat16),
        scratch_shapes=[pltpu.VMEM((rows, lanes), jnp.float32)],
        compiler_params=pltpu.CompilerParams(vmem_limit_bytes=24 << 20),
        cost_estimate=pl.CostEstimate(
            flops=4 * rows * (wq.size + wo.size),
            transcendentals=2 * rows * heads * width,
            bytes_accessed=4 * (wq.size + wo.size) + 4 * rows * lanes,
        ),
    )(place, state, wq, wo, memory, other_memory, *query_side, *output_side)


def partner(x, axis, flip):
    return lax.ppermute(x, axis, [(i, i ^ flip) for i in range(lax.axis_size(axis))])


def combine_kernel(heads, coef_ref, total_ref, got_ref, prior_ref, new_total_ref, new_prior_ref):
    for h in range(heads):
        got = got_ref[h].astype(jnp.float32)
        new_total_ref[h] = (
            coef_ref[0, h] * total_ref[h].astype(jnp.float32) + coef_ref[1, h] * got
        ).astype(jnp.bfloat16)
        new_prior_ref[h] = (coef_ref[2, h] * got + prior_ref[h].astype(jnp.float32)).astype(jnp.bfloat16)


def combine(coef, total, got, prior):
    vmem = pl.BlockSpec(memory_space=pltpu.VMEM)
    return pl.pallas_call(
        functools.partial(combine_kernel, total.shape[0]),
        in_specs=[pl.BlockSpec(memory_space=pltpu.SMEM)] + [vmem] * 3,
        out_specs=[vmem] * 2,
        out_shape=[jax.ShapeDtypeStruct(total.shape, jnp.bfloat16)] * 2,
        compiler_params=pltpu.CompilerParams(vmem_limit_bytes=8 << 20),
        cost_estimate=pl.CostEstimate(flops=4 * total.size, transcendentals=0, bytes_accessed=10 * total.size),
    )(coef, total, got, prior)


def scan_levels(decay, axis):
    count, me = lax.axis_size(axis), lax.axis_index(axis)
    order = jnp.arange(count)
    levels = []
    level = 1
    while level < count:
        mine = (order // level) == (me // level)
        theirs = (order // level) == ((me ^ level) // level)

        def product(mask):
            return jnp.prod(jnp.where(mask[:, None], decay, 1.0), axis=0)

        later = (me & level) != 0
        one = jnp.ones_like(decay[0])
        levels.append(
            (
                level,
                jnp.stack(
                    [
                        jnp.where(later, one, product(theirs)),
                        jnp.where(later, product(mine), one),
                        jnp.where(later, product(mine & (order < me)), 0.0 * one),
                    ]
                ),
            )
        )
        level *= 2
    return levels


def scan_memory(own, levels, axis, beside):
    total, prior = own, jnp.zeros_like(own)
    for level, coef in levels[:-1]:
        total, prior = combine(coef, total, partner(total, axis, level), prior)
    got = partner(total, axis, levels[-1][0])
    got, extra = lax.optimization_barrier((got, beside(total)))
    return total, got, prior, extra


def widen(held, axis, flip):
    return held + [partner(piece, axis, flip) for piece in held]


def after(value, *events):
    return lax.optimization_barrier((value, events))[0]


def slice_index(stages):
    place = jnp.int32(0)
    for k, (axis, flip) in enumerate(stages):
        place += jnp.where((lax.axis_index(axis) & flip) != 0, 1 << k, 0).astype(jnp.int32)
    return place


def tree_sum(terms):
    while len(terms) > 1:
        terms = [terms[i] + terms[i + 1] for i in range(0, len(terms), 2)]
    return terms[0]


def wide_sum(terms):
    return tree_sum([t.astype(jnp.float32) for t in terms])


def on_device(queries, keys, values, decay, gate, summary, wq_sum, wo_sum):
    heads = gate.shape[0]
    width = queries.shape[1] // heads
    model = summary.shape[1]
    parts, me = lax.axis_size("sub"), lax.axis_index("sub")
    rows = summary.shape[0] // parts

    flips = tuple((k << 1) | (k.bit_count() & 1) for k in range(parts // 2))

    depth = model >> len(QUERY_STAGES)
    place = jnp.stack([slice_index(QUERY_STAGES), slice_index(OUTPUT_STAGES)])
    own, query_block, output_block = memory_update(
        place, keys, values, wq_sum, wo_sum, depth, heads, width
    )
    query_block = partner(query_block, "sub", 1)
    output_block = partner(output_block, "sub", 1)

    levels = scan_levels(decay, "seq")

    def scan():
        return scan_memory(
            own, levels, "seq", lambda event: lifted_query(after(summary, event), wq_sum)
        )

    def skip():
        empty = jnp.zeros((heads, width + PAD, width), jnp.bfloat16)
        return empty, empty, empty, jnp.zeros((summary.shape[0], heads * width), jnp.bfloat16)

    total, got, early, lifted = lax.cond(gate[0] == gate[0], scan, skip)

    chunk = 512

    def fill(event, attended, *places):
        for first, head, count in places:
            attended = attention_piece(
                queries, keys, values, prior, after(gate, event), attended, width, first, chunk, head, count
            )
        return attended

    def swap(array, flip):
        order = [flips.index(f ^ flip) for f in flips]
        return jnp.concatenate([array[k * rows : (k + 1) * rows] for k in order], axis=0)

    def exchange(partial):
        return [partial] + [partner(partial, "sub", f) for f in flips[1:]]

    def summed(state, terms):
        terms = [terms[0]] + [swap(t, f) for t, f in zip(terms[1:], flips[1:])]
        return (state.astype(jnp.float32) + wide_sum(terms)).astype(jnp.bfloat16)

    state, kept, sent, final, prior = first_step(
        me.reshape(1), levels[-1][1], summary, lifted, total, got, early, wo_sum, heads, width, parts, flips
    )
    got = partner(sent, "sub", 1)
    query_other = partner(after(query_block, kept), *QUERY_STAGES[0])
    output_other = partner(after(output_block, kept), *OUTPUT_STAGES[0])
    other_final = partner(after(final, kept), "sub", 1)
    partial = wide_sum([kept, got]).astype(jnp.bfloat16)
    terms = exchange(partial)
    attended = fill(partial, None, (chunk, 0, heads))
    terms, attended, query_other, output_other, other_final = lax.optimization_barrier(
        (terms, attended, query_other, output_other, other_final)
    )
    query_side = widen([query_block, query_other], *QUERY_STAGES[1])
    output_side = widen([output_block, output_other], *OUTPUT_STAGES[1])
    attended = fill(terms[0], attended, (0, 0, heads))
    query_side, output_side, attended = lax.optimization_barrier((query_side, output_side, attended))
    state = summed(state, terms)

    last = [[(3 * chunk, 0, heads)], [(2 * chunk, 0, heads)], []]
    for step in range(1, STEPS):
        partial = wide_step(
            place, state, wq_sum, wo_sum, final, query_side, output_side, other_final, heads, width
        )
        terms = exchange(partial)
        attended = fill(partial, attended, *last[step - 1])
        terms, attended = lax.optimization_barrier((terms, attended))
        state = summed(state, terms)

    other = partner(state, "sub", 1)
    out = jnp.zeros_like(summary)
    for k, f in enumerate(flips):
        out = lax.dynamic_update_slice_in_dim(out, state[k * rows : (k + 1) * rows], (me ^ f) * rows, 0)
        out = lax.dynamic_update_slice_in_dim(out, other[k * rows : (k + 1) * rows], (me ^ f ^ 1) * rows, 0)
    return (attended, out)


def solution(mesh):
    placed = (
        P(("book", "seq"), "sub"),
        P(("book", "seq"), "sub"),
        P(("book", "seq"), "sub"),
        P("book", "sub"),
        P("sub"),
        P(("book", "seq"), None),
        P(None, "sub"),
        P("sub", None),
    )
    return jax.shard_map(
        on_device,
        mesh=mesh,
        in_specs=placed,
        out_specs=(P(("book", "seq"), "sub"), P(("book", "seq"), None)),
        check_vma=False,
    )
```

```python
import functools

import jax
import jax.numpy as jnp
from jax import lax
from jax.experimental import pallas as pl
from jax.experimental.pallas import tpu as pltpu
from jax.sharding import PartitionSpec as P

SEG = 2048
STEPS = 4
EPS = 1e-06
LOG2E = 1.4426950408889634
PAD = 16
UPDATE_ROWS = 512
QUERY_STAGES = (("book", 1), ("seq", 1))
OUTPUT_STAGES = (("seq", 2), ("seq", 1))


def lift(x):
    return jnp.where(x > 0.0, x + 1.0, jnp.exp(jnp.minimum(x, 0.0)))


def dot(a, b, dims):
    return lax.dot_general(a, b, (dims, ((), ())), preferred_element_type=jnp.float32)


def slice_kernel(depth, pieces, place_ref, wq_hbm, wo_hbm, query_hbm, output_hbm, query_ref, output_ref, sems):
    at = [pl.multiple_of(place_ref[i] * depth, depth) for i in range(2)]
    tall, wide = depth // pieces, wo_hbm.shape[0] // pieces
    moves = []
    for i in range(pieces):
        part, block = pl.ds(i * tall, tall), pl.ds(i * wide, wide)
        moves.append(
            (
                pltpu.make_async_copy(wq_hbm.at[pl.ds(at[0] + i * tall, tall)], query_ref.at[part], sems.at[4 * i]),
                pltpu.make_async_copy(query_ref.at[part], query_hbm.at[part], sems.at[4 * i + 1]),
            )
        )
        moves.append(
            (
                pltpu.make_async_copy(wo_hbm.at[block, pl.ds(at[1], depth)], output_ref.at[block], sems.at[4 * i + 2]),
                pltpu.make_async_copy(output_ref.at[block], output_hbm.at[block], sems.at[4 * i + 3]),
            )
        )
    for fetch, _ in moves:
        fetch.start()
    for fetch, back in moves:
        fetch.wait()
        back.start()
    for _, back in moves:
        back.wait()


def weight_slices(place, wq, wo, depth):
    pieces = 4
    hbm = pl.BlockSpec(memory_space=pltpu.HBM)
    shapes = ((depth, wq.shape[1]), (wo.shape[0], depth))
    return pl.pallas_call(
        functools.partial(slice_kernel, depth, pieces),
        in_specs=[pl.BlockSpec(memory_space=pltpu.SMEM), hbm, hbm],
        out_specs=[hbm, hbm],
        out_shape=[jax.ShapeDtypeStruct(shape, wq.dtype) for shape in shapes],
        scratch_shapes=[pltpu.VMEM(shape, wq.dtype) for shape in shapes] + [pltpu.SemaphoreType.DMA((4 * pieces,))],
        compiler_params=pltpu.CompilerParams(vmem_limit_bytes=60 << 20),
    )(place, wq, wo)


def update_kernel(heads, width, block, k_hbm, v_hbm, u_ref, k_ref, v_ref, acc, norm, sems):
    count = k_hbm.shape[0] // block
    copies = []
    for i in range(count):
        part = pl.ds(i * block, block)
        pair = (
            pltpu.make_async_copy(k_hbm.at[part], k_ref.at[part], sems.at[2 * i]),
            pltpu.make_async_copy(v_hbm.at[part], v_ref.at[part], sems.at[2 * i + 1]),
        )
        pair[0].start()
        pair[1].start()
        copies.append(pair)
    for i in range(count):
        part = slice(i * block, (i + 1) * block)
        copies[i][0].wait()
        copies[i][1].wait()
        for h in range(heads):
            cols = slice(h * width, (h + 1) * width)
            lifted = lift(k_ref[part, cols].astype(jnp.float32))
            total = jnp.sum(lifted, axis=0, keepdims=True)
            product = dot(lifted.astype(jnp.bfloat16), v_ref[part, cols], ((0,), (0,)))
            if i == 0:
                norm[h, 0:1, :] = total
                acc[h] = product
            else:
                norm[h, 0:1, :] += total
                acc[h] += product
    for h in range(heads):
        u_ref[h, :width, :] = acc[h].astype(jnp.bfloat16)
        u_ref[h, width:, :] = jnp.broadcast_to(norm[h, 0:1, :], (PAD, width)).astype(jnp.bfloat16)


def memory_update(keys, values, heads, width):
    rows, lanes = keys.shape
    count = rows // UPDATE_ROWS
    hbm = pl.BlockSpec(memory_space=pltpu.HBM)
    return pl.pallas_call(
        functools.partial(update_kernel, heads, width, UPDATE_ROWS),
        in_specs=[hbm, hbm],
        out_specs=pl.BlockSpec(memory_space=pltpu.VMEM),
        out_shape=jax.ShapeDtypeStruct((heads, width + PAD, width), jnp.bfloat16),
        scratch_shapes=[
            pltpu.VMEM((rows, lanes), jnp.bfloat16),
            pltpu.VMEM((rows, lanes), jnp.bfloat16),
            pltpu.VMEM((heads, width, width), jnp.float32),
            pltpu.VMEM((heads, 8, width), jnp.float32),
            pltpu.SemaphoreType.DMA((2 * count,)),
        ],
        compiler_params=pltpu.CompilerParams(vmem_limit_bytes=12 << 20),
        cost_estimate=pl.CostEstimate(
            flops=2 * rows * heads * width * width,
            transcendentals=rows * heads * width,
            bytes_accessed=4 * rows * heads * width,
        ),
    )(keys, values)


def lifted_query(state, wq):
    rows, depth = state.shape
    block = depth // 4
    return pl.pallas_call(
        query_kernel,
        grid=(4,),
        in_specs=[pl.BlockSpec((rows, block), lambda i: (0, i)), pl.BlockSpec((block, wq.shape[1]), lambda i: (i, 0))],
        out_specs=pl.BlockSpec((rows, wq.shape[1]), lambda i: (0, 0)),
        out_shape=jax.ShapeDtypeStruct((rows, wq.shape[1]), jnp.bfloat16),
        scratch_shapes=[pltpu.VMEM((rows, wq.shape[1]), jnp.float32)],
        compiler_params=pltpu.CompilerParams(vmem_limit_bytes=8 << 20),
        cost_estimate=pl.CostEstimate(
            flops=2 * rows * wq.size, transcendentals=rows * wq.shape[1], bytes_accessed=2 * wq.size
        ),
    )(state, wq)


def query_kernel(s_ref, w_ref, o_ref, acc):
    product = dot(s_ref[...], w_ref[...], ((1,), (0,)))

    @pl.when(pl.program_id(0) == 0)
    def _():
        acc[...] = product

    @pl.when(pl.program_id(0) != 0)
    def _():
        acc[...] += product

    @pl.when(pl.program_id(0) == pl.num_programs(0) - 1)
    def _():
        o_ref[...] = lift(acc[...]).astype(jnp.bfloat16)


def attention_kernel(heads, head, width, first, rows, tile, gate_ref, q_ref, k_ref, v_ref, m_ref, *rest):
    o_ref = rest[-1]
    at = first if q_ref.shape[0] > rows else 0
    factor = LOG2E * width ** (-0.5)
    blocks = (first + rows) // tile
    row = lax.broadcasted_iota(jnp.int32, (rows, tile), 0)
    col = lax.broadcasted_iota(jnp.int32, (rows, tile), 1)
    for h in range(head, head + heads):
        cols = slice(h * width, (h + 1) * width)
        q = q_ref[at : at + rows, cols]
        scores = []
        for j in range(blocks):
            s = dot(q, k_ref[j * tile : (j + 1) * tile, cols], ((1,), (1,))) * factor
            if (j + 1) * tile > first + 1:
                s = jnp.where(col + j * tile <= row + first, s, -jnp.inf)
            scores.append(s)
        top = scores[0]
        for s in scores[1:]:
            top = jnp.maximum(top, s)
        top = jnp.max(top, axis=1, keepdims=True)
        total = jnp.zeros((rows, 1), jnp.float32)
        mixed = jnp.zeros((rows, width), jnp.float32)
        for j in range(blocks):
            p = jnp.exp2(scores[j] - top)
            total += jnp.sum(p, axis=1, keepdims=True)
            mixed += dot(p.astype(jnp.bfloat16), v_ref[j * tile : (j + 1) * tile, cols], ((1,), (0,)))
        lifted = lift(q.astype(jnp.float32)).astype(jnp.bfloat16)
        numerator = dot(lifted, m_ref[h, :width, :], ((1,), (0,)))
        norm = m_ref[h, width : width + 1, :].astype(jnp.float32)
        denominator = jnp.sum(lifted.astype(jnp.float32) * norm, axis=1, keepdims=True) + 1.0
        blend = 1.0 / (1.0 + jnp.exp(jnp.full((1, 1), -gate_ref[h], jnp.float32)))
        mixed = mixed * ((1.0 - blend) / total) + numerator * (blend / denominator)
        mean = jnp.mean(mixed * mixed, axis=1, keepdims=True)
        out = slice((h - head) * width, (h - head + 1) * width)
        o_ref[:, out] = (mixed * lax.rsqrt(mean + EPS)).astype(jnp.bfloat16)


def attention_piece(q, k, v, memory, gate, out, width, first, rows, head, heads):
    lanes = heads * width
    span = first + rows
    vmem = pl.BlockSpec(memory_space=pltpu.VMEM)
    args = [gate, q, k, v, memory]
    specs = [pl.BlockSpec(memory_space=pltpu.SMEM)] + [vmem] * 4
    aliases = {}
    if True:
        specs[1] = pl.BlockSpec((rows, q.shape[1]), lambda i: (first // rows, 0))
        specs[2] = specs[3] = pl.BlockSpec((span, q.shape[1]), lambda i: (0, 0))
    if out is not None:
        args.append(out)
        specs.append(pl.BlockSpec(memory_space=pl.ANY))
        aliases = {5: 0}
    return pl.pallas_call(
        functools.partial(attention_kernel, heads, head, width, first, rows, 512),
        grid=(1,),
        in_specs=specs,
        out_specs=pl.BlockSpec((rows, lanes), lambda i: (first // rows, head // heads)),
        out_shape=jax.ShapeDtypeStruct(q.shape, jnp.bfloat16),
        input_output_aliases=aliases,
        compiler_params=pltpu.CompilerParams(vmem_limit_bytes=24 << 20),
        cost_estimate=pl.CostEstimate(
            flops=4 * rows * span * lanes,
            transcendentals=rows * span * heads,
            bytes_accessed=2 * lanes * (2 * rows + 2 * span),
        ),
    )(*args)


def read_memory(lifted, memory_ref, h, width):
    numerator = dot(lifted, memory_ref[h, :width, :], ((1,), (0,)))
    norm = memory_ref[h, width : width + 1, :].astype(jnp.float32)
    denominator = jnp.sum(lifted.astype(jnp.float32) * norm, axis=1, keepdims=True) + 1.0
    value = numerator / denominator
    mean = jnp.mean(value * value, axis=1, keepdims=True)
    return (value * lax.rsqrt(mean + EPS)).astype(jnp.bfloat16)


def read_heads(lifted, memory_ref, heads, width):
    return jnp.concatenate(
        [read_memory(lifted[:, h * width : (h + 1) * width], memory_ref, h, width) for h in range(heads)],
        axis=1,
    )


def first_kernel(
    heads, width, flips, parts, me_ref, coef_ref, state_ref, lifted_ref, total_ref, got_ref, early_ref, wo_hbm,
    half_ref, kept_ref, sent_ref, final_ref, prior_ref, wo_ref, acc, sems
):
    rows = state_ref.shape[0] // parts
    copies = []
    for h in range(heads):
        part = pl.ds(h * width, width)
        copies.append(pltpu.make_async_copy(wo_hbm.at[part], wo_ref.at[part], sems.at[h]))
        copies[h].start()
    combine_kernel(heads, coef_ref, total_ref, got_ref, early_ref, final_ref, prior_ref)
    for h in range(heads):
        part = slice(h * width, (h + 1) * width)
        read = read_memory(lifted_ref[:, part], final_ref, h, width)
        copies[h].wait()
        product = dot(read, wo_ref[part, :], ((1,), (0,)))
        acc[...] = product if h == 0 else acc[...] + product
    for k, f in enumerate(flips):
        at = pl.multiple_of((me_ref[0] ^ f) * rows, rows)
        half_ref[k * rows : (k + 1) * rows, :] = state_ref[pl.ds(at, rows), :]
        for j, ref in enumerate((kept_ref, sent_ref)):
            at = pl.multiple_of((me_ref[0] ^ j ^ f) * rows, rows)
            ref[k * rows : (k + 1) * rows, :] = acc[pl.ds(at, rows), :].astype(jnp.bfloat16)


def first_step(me, coef, state, lifted, total, got, early, wo, heads, width, parts, flips):
    rows, lanes = state.shape
    vmem, smem = pl.BlockSpec(memory_space=pltpu.VMEM), pl.BlockSpec(memory_space=pltpu.SMEM)
    shape = jax.ShapeDtypeStruct((rows // parts * len(flips), lanes), jnp.bfloat16)
    memory = jax.ShapeDtypeStruct(total.shape, jnp.bfloat16)
    return pl.pallas_call(
        functools.partial(first_kernel, heads, width, flips, parts),
        in_specs=[smem, smem] + [vmem] * 5 + [pl.BlockSpec(memory_space=pltpu.HBM)],
        out_specs=[vmem] * 5,
        out_shape=[shape] * 3 + [memory] * 2,
        scratch_shapes=[
            pltpu.VMEM(wo.shape, wo.dtype),
            pltpu.VMEM((rows, lanes), jnp.float32),
            pltpu.SemaphoreType.DMA((heads,)),
        ],
        compiler_params=pltpu.CompilerParams(vmem_limit_bytes=16 << 20),
        cost_estimate=pl.CostEstimate(
            flops=2 * rows * wo.size,
            transcendentals=rows * heads * width,
            bytes_accessed=2 * wo.size + 4 * rows * lanes,
        ),
    )(me, coef, state, lifted, total, got, early, wo)


def wide_kernel(heads, width, slices, place_ref, state_ref, wq_ref, wo_ref, m_ref, mx_ref, *rest):
    query_refs, output_refs, (out_ref, acc) = rest[:slices], rest[slices : 2 * slices], rest[2 * slices :]
    group = heads * width
    depth = state_ref.shape[1] // slices

    own = read_heads(lift(dot(state_ref[...], wq_ref[...], ((1,), (0,)))).astype(jnp.bfloat16), m_ref, heads, width)
    query = jnp.zeros((state_ref.shape[0], group), jnp.float32)
    for j in range(slices):
        at = pl.multiple_of((place_ref[0] ^ j) * depth, depth)
        query += dot(state_ref[:, pl.ds(at, depth)], query_refs[j][...], ((1,), (0,)))
    other = read_heads(lift(query).astype(jnp.bfloat16), mx_ref, heads, width)
    acc[...] = dot(own, wo_ref[...], ((1,), (0,)))
    for j in range(slices):
        at = pl.multiple_of((place_ref[1] ^ j) * depth, depth)
        acc[:, pl.ds(at, depth)] += dot(other, output_refs[j][...], ((1,), (0,)))
    out_ref[...] = acc[...].astype(jnp.bfloat16)


def wide_step(place, state, wq, wo, memory, query_side, output_side, other_memory, heads, width):
    rows, lanes = state.shape
    slices = len(query_side)
    vmem = pl.BlockSpec(memory_space=pltpu.VMEM)
    return pl.pallas_call(
        functools.partial(wide_kernel, heads, width, slices),
        in_specs=[pl.BlockSpec(memory_space=pltpu.SMEM)] + [vmem] * (5 + 2 * slices),
        out_specs=vmem,
        out_shape=jax.ShapeDtypeStruct((rows, lanes), jnp.bfloat16),
        scratch_shapes=[pltpu.VMEM((rows, lanes), jnp.float32)],
        compiler_params=pltpu.CompilerParams(vmem_limit_bytes=24 << 20),
        cost_estimate=pl.CostEstimate(
            flops=4 * rows * (wq.size + wo.size),
            transcendentals=2 * rows * heads * width,
            bytes_accessed=4 * (wq.size + wo.size) + 4 * rows * lanes,
        ),
    )(place, state, wq, wo, memory, other_memory, *query_side, *output_side)


def partner(x, axis, flip):
    return lax.ppermute(x, axis, [(i, i ^ flip) for i in range(lax.axis_size(axis))])


def combine_kernel(heads, coef_ref, total_ref, got_ref, prior_ref, new_total_ref, new_prior_ref):
    for h in range(heads):
        got = got_ref[h].astype(jnp.float32)
        new_total_ref[h] = (
            coef_ref[0, h] * total_ref[h].astype(jnp.float32) + coef_ref[1, h] * got
        ).astype(jnp.bfloat16)
        new_prior_ref[h] = (coef_ref[2, h] * got + prior_ref[h].astype(jnp.float32)).astype(jnp.bfloat16)


def combine(coef, total, got, prior):
    vmem = pl.BlockSpec(memory_space=pltpu.VMEM)
    return pl.pallas_call(
        functools.partial(combine_kernel, total.shape[0]),
        in_specs=[pl.BlockSpec(memory_space=pltpu.SMEM)] + [vmem] * 3,
        out_specs=[vmem] * 2,
        out_shape=[jax.ShapeDtypeStruct(total.shape, jnp.bfloat16)] * 2,
        compiler_params=pltpu.CompilerParams(vmem_limit_bytes=8 << 20),
        cost_estimate=pl.CostEstimate(flops=4 * total.size, transcendentals=0, bytes_accessed=10 * total.size),
    )(coef, total, got, prior)


def scan_levels(decay, axis):
    count, me = lax.axis_size(axis), lax.axis_index(axis)
    order = jnp.arange(count)
    levels = []
    level = 1
    while level < count:
        mine = (order // level) == (me // level)
        theirs = (order // level) == ((me ^ level) // level)

        def product(mask):
            return jnp.prod(jnp.where(mask[:, None], decay, 1.0), axis=0)

        later = (me & level) != 0
        one = jnp.ones_like(decay[0])
        levels.append(
            (
                level,
                jnp.stack(
                    [
                        jnp.where(later, one, product(theirs)),
                        jnp.where(later, product(mine), one),
                        jnp.where(later, product(mine & (order < me)), 0.0 * one),
                    ]
                ),
            )
        )
        level *= 2
    return levels


def scan_memory(own, levels, axis, beside):
    total, prior = own, jnp.zeros_like(own)
    for level, coef in levels[:-1]:
        total, prior = combine(coef, total, partner(total, axis, level), prior)
    got = partner(total, axis, levels[-1][0])
    got, extra = lax.optimization_barrier((got, beside(total)))
    return total, got, prior, extra


def widen(held, axis, flip):
    return held + [partner(piece, axis, flip) for piece in held]


def after(value, *events):
    return lax.optimization_barrier((value, events))[0]


def slice_index(stages):
    place = jnp.int32(0)
    for k, (axis, flip) in enumerate(stages):
        place += jnp.where((lax.axis_index(axis) & flip) != 0, 1 << k, 0).astype(jnp.int32)
    return place


def tree_sum(terms):
    while len(terms) > 1:
        terms = [terms[i] + terms[i + 1] for i in range(0, len(terms), 2)]
    return terms[0]


def wide_sum(terms):
    return tree_sum([t.astype(jnp.float32) for t in terms])


def on_device(queries, keys, values, decay, gate, summary, wq_sum, wo_sum):
    heads = gate.shape[0]
    width = queries.shape[1] // heads
    model = summary.shape[1]
    parts, me = lax.axis_size("sub"), lax.axis_index("sub")
    rows = summary.shape[0] // parts

    flips = tuple((k << 1) | (k.bit_count() & 1) for k in range(parts // 2))

    depth = model >> len(QUERY_STAGES)
    place = jnp.stack([slice_index(QUERY_STAGES), slice_index(OUTPUT_STAGES)])
    query_block, output_block = weight_slices(place, wq_sum, wo_sum, depth)
    query_block = partner(query_block, "sub", 1)
    output_block = partner(output_block, "sub", 1)

    levels = scan_levels(decay, "seq")

    def scan():
        own = memory_update(keys, values, heads, width)
        return scan_memory(
            own, levels, "seq", lambda event: lifted_query(after(summary, event), wq_sum)
        )

    def skip():
        empty = jnp.zeros((heads, width + PAD, width), jnp.bfloat16)
        return empty, empty, empty, jnp.zeros((summary.shape[0], heads * width), jnp.bfloat16)

    total, got, early, lifted = lax.cond(gate[0] == gate[0], scan, skip)

    chunk = 512

    def fill(event, attended, *places):
        for first, head, count in places:
            attended = attention_piece(
                queries, keys, values, prior, after(gate, event), attended, width, first, chunk, head, count
            )
        return attended

    def swap(array, flip):
        order = [flips.index(f ^ flip) for f in flips]
        return jnp.concatenate([array[k * rows : (k + 1) * rows] for k in order], axis=0)

    def exchange(partial):
        return [partial] + [partner(partial, "sub", f) for f in flips[1:]]

    def summed(state, terms):
        terms = [terms[0]] + [swap(t, f) for t, f in zip(terms[1:], flips[1:])]
        return (state.astype(jnp.float32) + wide_sum(terms)).astype(jnp.bfloat16)

    state, kept, sent, final, prior = first_step(
        me.reshape(1), levels[-1][1], summary, lifted, total, got, early, wo_sum, heads, width, parts, flips
    )
    got = partner(sent, "sub", 1)
    query_other = partner(after(query_block, kept), *QUERY_STAGES[0])
    output_other = partner(after(output_block, kept), *OUTPUT_STAGES[0])
    other_final = partner(after(final, kept), "sub", 1)
    partial = wide_sum([kept, got]).astype(jnp.bfloat16)
    terms = exchange(partial)
    attended = fill(partial, None, (chunk, 0, heads))
    terms, attended, query_other, output_other, other_final = lax.optimization_barrier(
        (terms, attended, query_other, output_other, other_final)
    )
    query_side = widen([query_block, query_other], *QUERY_STAGES[1])
    output_side = widen([output_block, output_other], *OUTPUT_STAGES[1])
    attended = fill(terms[0], attended, (0, 0, heads))
    query_side, output_side, attended = lax.optimization_barrier((query_side, output_side, attended))
    state = summed(state, terms)

    last = [[(3 * chunk, 0, heads)], [(2 * chunk, 0, heads)], []]
    for step in range(1, STEPS):
        partial = wide_step(
            place, state, wq_sum, wo_sum, final, query_side, output_side, other_final, heads, width
        )
        terms = exchange(partial)
        attended = fill(partial, attended, *last[step - 1])
        terms, attended = lax.optimization_barrier((terms, attended))
        state = summed(state, terms)

    other = partner(state, "sub", 1)
    out = jnp.zeros_like(summary)
    for k, f in enumerate(flips):
        out = lax.dynamic_update_slice_in_dim(out, state[k * rows : (k + 1) * rows], (me ^ f) * rows, 0)
        out = lax.dynamic_update_slice_in_dim(out, other[k * rows : (k + 1) * rows], (me ^ f ^ 1) * rows, 0)
    return (attended, out)


def solution(mesh):
    placed = (
        P(("book", "seq"), "sub"),
        P(("book", "seq"), "sub"),
        P(("book", "seq"), "sub"),
        P("book", "sub"),
        P("sub"),
        P(("book", "seq"), None),
        P(None, "sub"),
        P("sub", None),
    )
    return jax.shard_map(
        on_device,
        mesh=mesh,
        in_specs=placed,
        out_specs=(P(("book", "seq"), "sub"), P(("book", "seq"), None)),
        check_vma=False,
    )
```

```python
import functools

import jax
import jax.numpy as jnp
from jax import lax
from jax.experimental import pallas as pl
from jax.experimental.pallas import tpu as pltpu
from jax.sharding import PartitionSpec as P

SEG = 2048
STEPS = 4
EPS = 1e-06
LOG2E = 1.4426950408889634
PAD = 16
UPDATE_ROWS = 512
QUERY_STAGES = (("book", 1), ("seq", 1))
OUTPUT_STAGES = (("seq", 2), ("seq", 1))


def lift(x):
    return jnp.where(x > 0.0, x + 1.0, jnp.exp(jnp.minimum(x, 0.0)))


def dot(a, b, dims):
    return lax.dot_general(a, b, (dims, ((), ())), preferred_element_type=jnp.float32)


def slice_kernel(depth, pieces, wq_hbm, wo_hbm, query_hbm, output_hbm, query_ref, output_ref, sems):
    at = [pl.multiple_of(slice_index(stages) * depth, depth) for stages in (QUERY_STAGES, OUTPUT_STAGES)]
    tall, wide = depth // pieces, wo_hbm.shape[0] // pieces
    moves = []
    for i in range(pieces):
        part, block = pl.ds(i * tall, tall), pl.ds(i * wide, wide)
        moves.append(
            (
                pltpu.make_async_copy(wq_hbm.at[pl.ds(at[0] + i * tall, tall)], query_ref.at[part], sems.at[4 * i]),
                pltpu.make_async_copy(query_ref.at[part], query_hbm.at[part], sems.at[4 * i + 1]),
            )
        )
        moves.append(
            (
                pltpu.make_async_copy(wo_hbm.at[block, pl.ds(at[1], depth)], output_ref.at[block], sems.at[4 * i + 2]),
                pltpu.make_async_copy(output_ref.at[block], output_hbm.at[block], sems.at[4 * i + 3]),
            )
        )
    for fetch, _ in moves:
        fetch.start()
    for fetch, back in moves:
        fetch.wait()
        back.start()
    for _, back in moves:
        back.wait()


def weight_slices(wq, wo, depth):
    pieces = 4
    hbm = pl.BlockSpec(memory_space=pltpu.HBM)
    shapes = ((depth, wq.shape[1]), (wo.shape[0], depth))
    return pl.pallas_call(
        functools.partial(slice_kernel, depth, pieces),
        in_specs=[hbm, hbm],
        out_specs=[hbm, hbm],
        out_shape=[jax.ShapeDtypeStruct(shape, wq.dtype) for shape in shapes],
        scratch_shapes=[pltpu.VMEM(shape, wq.dtype) for shape in shapes] + [pltpu.SemaphoreType.DMA((4 * pieces,))],
        compiler_params=pltpu.CompilerParams(vmem_limit_bytes=60 << 20),
    )(wq, wo)


def update_kernel(heads, width, block, k_hbm, v_hbm, u_ref, k_ref, v_ref, acc, norm, sems):
    count = k_hbm.shape[0] // block
    copies = []
    for i in range(count):
        part = pl.ds(i * block, block)
        pair = (
            pltpu.make_async_copy(k_hbm.at[part], k_ref.at[part], sems.at[2 * i]),
            pltpu.make_async_copy(v_hbm.at[part], v_ref.at[part], sems.at[2 * i + 1]),
        )
        pair[0].start()
        pair[1].start()
        copies.append(pair)
    for i in range(count):
        part = slice(i * block, (i + 1) * block)
        copies[i][0].wait()
        copies[i][1].wait()
        for h in range(heads):
            cols = slice(h * width, (h + 1) * width)
            lifted = lift(k_ref[part, cols].astype(jnp.float32))
            total = jnp.sum(lifted, axis=0, keepdims=True)
            product = dot(lifted.astype(jnp.bfloat16), v_ref[part, cols], ((0,), (0,)))
            if i == 0:
                norm[h, 0:1, :] = total
                acc[h] = product
            else:
                norm[h, 0:1, :] += total
                acc[h] += product
    for h in range(heads):
        u_ref[h, :width, :] = acc[h].astype(jnp.bfloat16)
        u_ref[h, width:, :] = jnp.broadcast_to(norm[h, 0:1, :], (PAD, width)).astype(jnp.bfloat16)


def memory_update(keys, values, heads, width):
    rows, lanes = keys.shape
    count = rows // UPDATE_ROWS
    hbm = pl.BlockSpec(memory_space=pltpu.HBM)
    return pl.pallas_call(
        functools.partial(update_kernel, heads, width, UPDATE_ROWS),
        in_specs=[hbm, hbm],
        out_specs=pl.BlockSpec(memory_space=pltpu.VMEM),
        out_shape=jax.ShapeDtypeStruct((heads, width + PAD, width), jnp.bfloat16),
        scratch_shapes=[
            pltpu.VMEM((rows, lanes), jnp.bfloat16),
            pltpu.VMEM((rows, lanes), jnp.bfloat16),
            pltpu.VMEM((heads, width, width), jnp.float32),
            pltpu.VMEM((heads, 8, width), jnp.float32),
            pltpu.SemaphoreType.DMA((2 * count,)),
        ],
        compiler_params=pltpu.CompilerParams(vmem_limit_bytes=12 << 20),
        cost_estimate=pl.CostEstimate(
            flops=2 * rows * heads * width * width,
            transcendentals=rows * heads * width,
            bytes_accessed=4 * rows * heads * width,
        ),
    )(keys, values)


def lifted_query(state, wq):
    rows, depth = state.shape
    block = depth // 4
    return pl.pallas_call(
        query_kernel,
        grid=(4,),
        in_specs=[pl.BlockSpec((rows, block), lambda i: (0, i)), pl.BlockSpec((block, wq.shape[1]), lambda i: (i, 0))],
        out_specs=pl.BlockSpec((rows, wq.shape[1]), lambda i: (0, 0)),
        out_shape=jax.ShapeDtypeStruct((rows, wq.shape[1]), jnp.bfloat16),
        scratch_shapes=[pltpu.VMEM((rows, wq.shape[1]), jnp.float32)],
        compiler_params=pltpu.CompilerParams(vmem_limit_bytes=8 << 20),
        cost_estimate=pl.CostEstimate(
            flops=2 * rows * wq.size, transcendentals=rows * wq.shape[1], bytes_accessed=2 * wq.size
        ),
    )(state, wq)


def query_kernel(s_ref, w_ref, o_ref, acc):
    product = dot(s_ref[...], w_ref[...], ((1,), (0,)))

    @pl.when(pl.program_id(0) == 0)
    def _():
        acc[...] = product

    @pl.when(pl.program_id(0) != 0)
    def _():
        acc[...] += product

    @pl.when(pl.program_id(0) == pl.num_programs(0) - 1)
    def _():
        o_ref[...] = lift(acc[...]).astype(jnp.bfloat16)


def attention_kernel(heads, head, width, first, rows, tile, gate_ref, q_ref, k_ref, v_ref, m_ref, *rest):
    o_ref = rest[-1]
    at = first if q_ref.shape[0] > rows else 0
    factor = LOG2E * width ** (-0.5)
    blocks = (first + rows) // tile
    row = lax.broadcasted_iota(jnp.int32, (rows, tile), 0)
    col = lax.broadcasted_iota(jnp.int32, (rows, tile), 1)
    for h in range(head, head + heads):
        cols = slice(h * width, (h + 1) * width)
        q = q_ref[at : at + rows, cols]
        scores = []
        for j in range(blocks):
            s = dot(q, k_ref[j * tile : (j + 1) * tile, cols], ((1,), (1,))) * factor
            if (j + 1) * tile > first + 1:
                s = jnp.where(col + j * tile <= row + first, s, -jnp.inf)
            scores.append(s)
        top = scores[0]
        for s in scores[1:]:
            top = jnp.maximum(top, s)
        top = jnp.max(top, axis=1, keepdims=True)
        total = jnp.zeros((rows, 1), jnp.float32)
        mixed = jnp.zeros((rows, width), jnp.float32)
        for j in range(blocks):
            p = jnp.exp2(scores[j] - top)
            total += jnp.sum(p, axis=1, keepdims=True)
            mixed += dot(p.astype(jnp.bfloat16), v_ref[j * tile : (j + 1) * tile, cols], ((1,), (0,)))
        lifted = lift(q.astype(jnp.float32)).astype(jnp.bfloat16)
        numerator = dot(lifted, m_ref[h, :width, :], ((1,), (0,)))
        norm = m_ref[h, width : width + 1, :].astype(jnp.float32)
        denominator = jnp.sum(lifted.astype(jnp.float32) * norm, axis=1, keepdims=True) + 1.0
        blend = 1.0 / (1.0 + jnp.exp(jnp.full((1, 1), -gate_ref[h], jnp.float32)))
        mixed = mixed * ((1.0 - blend) / total) + numerator * (blend / denominator)
        mean = jnp.mean(mixed * mixed, axis=1, keepdims=True)
        out = slice((h - head) * width, (h - head + 1) * width)
        o_ref[:, out] = (mixed * lax.rsqrt(mean + EPS)).astype(jnp.bfloat16)


def attention_piece(q, k, v, memory, gate, out, width, first, rows, head, heads):
    lanes = heads * width
    span = first + rows
    vmem = pl.BlockSpec(memory_space=pltpu.VMEM)
    args = [gate, q, k, v, memory]
    specs = [pl.BlockSpec(memory_space=pltpu.SMEM)] + [vmem] * 4
    aliases = {}
    if True:
        specs[1] = pl.BlockSpec((rows, q.shape[1]), lambda i: (first // rows, 0))
        specs[2] = specs[3] = pl.BlockSpec((span, q.shape[1]), lambda i: (0, 0))
    if out is not None:
        args.append(out)
        specs.append(pl.BlockSpec(memory_space=pl.ANY))
        aliases = {5: 0}
    return pl.pallas_call(
        functools.partial(attention_kernel, heads, head, width, first, rows, 512),
        grid=(1,),
        in_specs=specs,
        out_specs=pl.BlockSpec((rows, lanes), lambda i: (first // rows, head // heads)),
        out_shape=jax.ShapeDtypeStruct(q.shape, jnp.bfloat16),
        input_output_aliases=aliases,
        compiler_params=pltpu.CompilerParams(vmem_limit_bytes=24 << 20),
        cost_estimate=pl.CostEstimate(
            flops=4 * rows * span * lanes,
            transcendentals=rows * span * heads,
            bytes_accessed=2 * lanes * (2 * rows + 2 * span),
        ),
    )(*args)


def read_memory(lifted, memory_ref, h, width):
    numerator = dot(lifted, memory_ref[h, :width, :], ((1,), (0,)))
    norm = memory_ref[h, width : width + 1, :].astype(jnp.float32)
    denominator = jnp.sum(lifted.astype(jnp.float32) * norm, axis=1, keepdims=True) + 1.0
    value = numerator / denominator
    mean = jnp.mean(value * value, axis=1, keepdims=True)
    return (value * lax.rsqrt(mean + EPS)).astype(jnp.bfloat16)


def read_heads(lifted, memory_ref, heads, width):
    return jnp.concatenate(
        [read_memory(lifted[:, h * width : (h + 1) * width], memory_ref, h, width) for h in range(heads)],
        axis=1,
    )


def first_kernel(
    heads, width, flips, parts, me_ref, coef_ref, state_ref, lifted_ref, total_ref, got_ref, early_ref, wo_hbm,
    half_ref, kept_ref, sent_ref, final_ref, prior_ref, wo_ref, acc, sems
):
    rows = state_ref.shape[0] // parts
    copies = []
    for h in range(heads):
        part = pl.ds(h * width, width)
        copies.append(pltpu.make_async_copy(wo_hbm.at[part], wo_ref.at[part], sems.at[h]))
        copies[h].start()
    combine_kernel(heads, coef_ref, total_ref, got_ref, early_ref, final_ref, prior_ref)
    for h in range(heads):
        part = slice(h * width, (h + 1) * width)
        read = read_memory(lifted_ref[:, part], final_ref, h, width)
        copies[h].wait()
        product = dot(read, wo_ref[part, :], ((1,), (0,)))
        acc[...] = product if h == 0 else acc[...] + product
    for k, f in enumerate(flips):
        at = pl.multiple_of((me_ref[0] ^ f) * rows, rows)
        half_ref[k * rows : (k + 1) * rows, :] = state_ref[pl.ds(at, rows), :]
        for j, ref in enumerate((kept_ref, sent_ref)):
            at = pl.multiple_of((me_ref[0] ^ j ^ f) * rows, rows)
            ref[k * rows : (k + 1) * rows, :] = acc[pl.ds(at, rows), :].astype(jnp.bfloat16)


def first_step(me, coef, state, lifted, total, got, early, wo, heads, width, parts, flips):
    rows, lanes = state.shape
    vmem, smem = pl.BlockSpec(memory_space=pltpu.VMEM), pl.BlockSpec(memory_space=pltpu.SMEM)
    shape = jax.ShapeDtypeStruct((rows // parts * len(flips), lanes), jnp.bfloat16)
    memory = jax.ShapeDtypeStruct(total.shape, jnp.bfloat16)
    return pl.pallas_call(
        functools.partial(first_kernel, heads, width, flips, parts),
        in_specs=[smem, smem] + [vmem] * 5 + [pl.BlockSpec(memory_space=pltpu.HBM)],
        out_specs=[vmem] * 5,
        out_shape=[shape] * 3 + [memory] * 2,
        scratch_shapes=[
            pltpu.VMEM(wo.shape, wo.dtype),
            pltpu.VMEM((rows, lanes), jnp.float32),
            pltpu.SemaphoreType.DMA((heads,)),
        ],
        compiler_params=pltpu.CompilerParams(vmem_limit_bytes=16 << 20),
        cost_estimate=pl.CostEstimate(
            flops=2 * rows * wo.size,
            transcendentals=rows * heads * width,
            bytes_accessed=2 * wo.size + 4 * rows * lanes,
        ),
    )(me, coef, state, lifted, total, got, early, wo)


def wide_kernel(heads, width, slices, state_ref, wq_ref, wo_ref, m_ref, mx_ref, *rest):
    query_refs, output_refs, (out_ref, acc) = rest[:slices], rest[slices : 2 * slices], rest[2 * slices :]
    group = heads * width
    depth = state_ref.shape[1] // slices

    own = read_heads(lift(dot(state_ref[...], wq_ref[...], ((1,), (0,)))).astype(jnp.bfloat16), m_ref, heads, width)
    query = jnp.zeros((state_ref.shape[0], group), jnp.float32)
    for j in range(slices):
        at = pl.multiple_of((slice_index(QUERY_STAGES) ^ j) * depth, depth)
        query += dot(state_ref[:, pl.ds(at, depth)], query_refs[j][...], ((1,), (0,)))
    other = read_heads(lift(query).astype(jnp.bfloat16), mx_ref, heads, width)
    acc[...] = dot(own, wo_ref[...], ((1,), (0,)))
    for j in range(slices):
        at = pl.multiple_of((slice_index(OUTPUT_STAGES) ^ j) * depth, depth)
        acc[:, pl.ds(at, depth)] += dot(other, output_refs[j][...], ((1,), (0,)))
    out_ref[...] = acc[...].astype(jnp.bfloat16)


def wide_step(state, wq, wo, memory, query_side, output_side, other_memory, heads, width):
    rows, lanes = state.shape
    slices = len(query_side)
    vmem = pl.BlockSpec(memory_space=pltpu.VMEM)
    return pl.pallas_call(
        functools.partial(wide_kernel, heads, width, slices),
        in_specs=[vmem] * (5 + 2 * slices),
        out_specs=vmem,
        out_shape=jax.ShapeDtypeStruct((rows, lanes), jnp.bfloat16),
        scratch_shapes=[pltpu.VMEM((rows, lanes), jnp.float32)],
        compiler_params=pltpu.CompilerParams(vmem_limit_bytes=24 << 20),
        cost_estimate=pl.CostEstimate(
            flops=4 * rows * (wq.size + wo.size),
            transcendentals=2 * rows * heads * width,
            bytes_accessed=4 * (wq.size + wo.size) + 4 * rows * lanes,
        ),
    )(state, wq, wo, memory, other_memory, *query_side, *output_side)


def partner(x, axis, flip):
    return lax.ppermute(x, axis, [(i, i ^ flip) for i in range(lax.axis_size(axis))])


def combine_kernel(heads, coef_ref, total_ref, got_ref, prior_ref, new_total_ref, new_prior_ref):
    for h in range(heads):
        got = got_ref[h].astype(jnp.float32)
        new_total_ref[h] = (
            coef_ref[0, h] * total_ref[h].astype(jnp.float32) + coef_ref[1, h] * got
        ).astype(jnp.bfloat16)
        new_prior_ref[h] = (coef_ref[2, h] * got + prior_ref[h].astype(jnp.float32)).astype(jnp.bfloat16)


def combine(coef, total, got, prior):
    vmem = pl.BlockSpec(memory_space=pltpu.VMEM)
    return pl.pallas_call(
        functools.partial(combine_kernel, total.shape[0]),
        in_specs=[pl.BlockSpec(memory_space=pltpu.SMEM)] + [vmem] * 3,
        out_specs=[vmem] * 2,
        out_shape=[jax.ShapeDtypeStruct(total.shape, jnp.bfloat16)] * 2,
        compiler_params=pltpu.CompilerParams(vmem_limit_bytes=8 << 20),
        cost_estimate=pl.CostEstimate(flops=4 * total.size, transcendentals=0, bytes_accessed=10 * total.size),
    )(coef, total, got, prior)


def scan_levels(decay, axis):
    count, me = lax.axis_size(axis), lax.axis_index(axis)
    order = jnp.arange(count)
    levels = []
    level = 1
    while level < count:
        mine = (order // level) == (me // level)
        theirs = (order // level) == ((me ^ level) // level)

        def product(mask):
            return jnp.prod(jnp.where(mask[:, None], decay, 1.0), axis=0)

        later = (me & level) != 0
        one = jnp.ones_like(decay[0])
        levels.append(
            (
                level,
                jnp.stack(
                    [
                        jnp.where(later, one, product(theirs)),
                        jnp.where(later, product(mine), one),
                        jnp.where(later, product(mine & (order < me)), 0.0 * one),
                    ]
                ),
            )
        )
        level *= 2
    return levels


def scan_memory(own, levels, axis, beside):
    total, prior = own, jnp.zeros_like(own)
    for level, coef in levels[:-1]:
        total, prior = combine(coef, total, partner(total, axis, level), prior)
    got = partner(total, axis, levels[-1][0])
    got, extra = lax.optimization_barrier((got, beside(total)))
    return total, got, prior, extra


def widen(held, axis, flip):
    return held + [partner(piece, axis, flip) for piece in held]


def after(value, *events):
    return lax.optimization_barrier((value, events))[0]


def slice_index(stages):
    place = jnp.int32(0)
    for k, (axis, flip) in enumerate(stages):
        place += jnp.where((lax.axis_index(axis) & flip) != 0, 1 << k, 0).astype(jnp.int32)
    return place


def tree_sum(terms):
    while len(terms) > 1:
        terms = [terms[i] + terms[i + 1] for i in range(0, len(terms), 2)]
    return terms[0]


def wide_sum(terms):
    return tree_sum([t.astype(jnp.float32) for t in terms])


def on_device(queries, keys, values, decay, gate, summary, wq_sum, wo_sum):
    heads = gate.shape[0]
    width = queries.shape[1] // heads
    model = summary.shape[1]
    parts, me = lax.axis_size("sub"), lax.axis_index("sub")
    rows = summary.shape[0] // parts

    flips = tuple((k << 1) | (k.bit_count() & 1) for k in range(parts // 2))

    depth = model >> len(QUERY_STAGES)
    query_block, output_block = weight_slices(wq_sum, wo_sum, depth)
    query_block = partner(query_block, "sub", 1)
    output_block = partner(output_block, "sub", 1)

    levels = scan_levels(decay, "seq")

    def scan():
        own = memory_update(keys, values, heads, width)
        return scan_memory(
            own, levels, "seq", lambda event: lifted_query(after(summary, event), wq_sum)
        )

    def skip():
        empty = jnp.zeros((heads, width + PAD, width), jnp.bfloat16)
        return empty, empty, empty, jnp.zeros((summary.shape[0], heads * width), jnp.bfloat16)

    total, got, early, lifted = lax.cond(gate[0] == gate[0], scan, skip)

    chunk = 512

    def fill(event, attended, *places):
        for first, head, count in places:
            attended = attention_piece(
                queries, keys, values, prior, after(gate, event), attended, width, first, chunk, head, count
            )
        return attended

    def swap(array, flip):
        order = [flips.index(f ^ flip) for f in flips]
        return jnp.concatenate([array[k * rows : (k + 1) * rows] for k in order], axis=0)

    def exchange(partial):
        return [partial] + [partner(partial, "sub", f) for f in flips[1:]]

    def summed(state, terms):
        terms = [terms[0]] + [swap(t, f) for t, f in zip(terms[1:], flips[1:])]
        return (state.astype(jnp.float32) + wide_sum(terms)).astype(jnp.bfloat16)

    state, kept, sent, final, prior = first_step(
        me.reshape(1), levels[-1][1], summary, lifted, total, got, early, wo_sum, heads, width, parts, flips
    )
    got = partner(sent, "sub", 1)
    query_other = partner(after(query_block, kept), *QUERY_STAGES[0])
    output_other = partner(after(output_block, kept), *OUTPUT_STAGES[0])
    other_final = partner(after(final, kept), "sub", 1)
    partial = wide_sum([kept, got]).astype(jnp.bfloat16)
    terms = exchange(partial)
    attended = fill(partial, None, (chunk, 0, heads))
    terms, attended, query_other, output_other, other_final = lax.optimization_barrier(
        (terms, attended, query_other, output_other, other_final)
    )
    query_side = widen([query_block, query_other], *QUERY_STAGES[1])
    output_side = widen([output_block, output_other], *OUTPUT_STAGES[1])
    attended = fill(terms[0], attended, (0, 0, heads))
    query_side, output_side, attended = lax.optimization_barrier((query_side, output_side, attended))
    state = summed(state, terms)

    last = [[(3 * chunk, 0, heads)], [(2 * chunk, 0, heads)], []]
    for step in range(1, STEPS):
        partial = wide_step(
            state, wq_sum, wo_sum, final, query_side, output_side, other_final, heads, width
        )
        terms = exchange(partial)
        attended = fill(partial, attended, *last[step - 1])
        terms, attended = lax.optimization_barrier((terms, attended))
        state = summed(state, terms)

    other = partner(state, "sub", 1)
    out = jnp.zeros_like(summary)
    for k, f in enumerate(flips):
        out = lax.dynamic_update_slice_in_dim(out, state[k * rows : (k + 1) * rows], (me ^ f) * rows, 0)
        out = lax.dynamic_update_slice_in_dim(out, other[k * rows : (k + 1) * rows], (me ^ f ^ 1) * rows, 0)
    return (attended, out)


def solution(mesh):
    placed = (
        P(("book", "seq"), "sub"),
        P(("book", "seq"), "sub"),
        P(("book", "seq"), "sub"),
        P("book", "sub"),
        P("sub"),
        P(("book", "seq"), None),
        P(None, "sub"),
        P("sub", None),
    )
    return jax.shard_map(
        on_device,
        mesh=mesh,
        in_specs=placed,
        out_specs=(P(("book", "seq"), "sub"), P(("book", "seq"), None)),
        check_vma=False,
    )
```
